256 devices in a mesh: half: 2 (over core), row: 8 (over z_hi, x), col: 16 (over y, z_lo).
Axes of the slice: x: 4, y: 4, z: 8 (z_hi: 2, z_lo: 4; z = z_hi * 4 + z_lo), core: 2. Of those that a mesh axis runs over, the one named last changes fastest.
Arguments:
- parent_front: float32 [16384, 16384], P(('half', 'row'), 'col'), may hold values from -6 to 6
- child_blocks: float32 [2, 8192, 8192], P('half', 'row', 'col'), may hold values from -6 to 6
- row_maps: int32 [2, 8192], replicated, may hold values from 0 to 16383, as said below
- inverse_blocks: float32 [4, 128, 128], replicated, may hold values from -0.12 to 0.12
Outputs:
- updated_front: float32 [16384, 16384], P(('half', 'row'), 'col')
- panel_factor: bfloat16 [16384, 512], P(('half', 'row'))
The draws below stay inside these ranges and needn't reach their ends.
Inputs may be any that keep to these rules, and one draw needn't show every extreme that they name: `row_maps`: each row lists 8192 distinct parent rows. In every aligned block of 512 entries of a row, at most 64 entries fall in one aligned block of 1024 parent rows, and that bound is reached in every such block; in every aligned block of 1024 entries, at most 128 fall in one aligned block of 1024 parent rows, and that bound is reached in every such block.
All inputs are finite; a program needn't handle non-finite values.
Results may differ from the reference program's by a relative error of at most 0.001.
Values sent between devices are 32-bit elements; how exact they have to be, the bound alone decides.
A program may use at most 128 MiB of HBM per device.

```python
import jax
import jax.numpy as jnp
from jax import lax

CHILD = 8192
PB = 128
NPB = 4
PARENT = 16384
GROUPS = 16
ROW_SHARD = 1024
COL_SHARD = 512
COL_LOC = 1024


def child_map(key):
    blocks = CHILD // COL_SHARD
    colgroups = PARENT // COL_LOC
    span = colgroups // GROUPS
    base = COL_SHARD // colgroups
    shards = CHILD // ROW_SHARD
    within = ROW_SHARD // COL_SHARD
    key_hot, key_cold, key_order, key_place = jax.random.split(key, 4)
    hottest = jnp.repeat(jax.random.randint(key_hot, (shards,), 0, colgroups), within)
    offset = jax.random.randint(key_cold, (blocks,), 0, colgroups - span)
    coldest = (hottest // span * span + span + offset) % colgroups
    labels_all = jnp.arange(colgroups, dtype=jnp.int32)
    counts = base + base * (hottest[:, None] == labels_all).astype(jnp.int32) - base * (coldest[:, None] == labels_all).astype(jnp.int32)
    bounds = jnp.cumsum(counts, axis=1)
    position = jnp.arange(COL_SHARD, dtype=jnp.int32)
    sorted_labels = jnp.sum((position[None, :, None] >= bounds[:, None, :]).astype(jnp.int32), axis=2)
    orders = jax.vmap(lambda subkey: jax.random.permutation(subkey, COL_SHARD))(jax.random.split(key_order, blocks))
    labels = jnp.take_along_axis(sorted_labels, orders, axis=1).reshape(CHILD)
    onehot = (labels[:, None] == labels_all).astype(jnp.int32)
    rank = jnp.sum((jnp.cumsum(onehot, axis=0) - onehot) * onehot, axis=1)
    places = jax.vmap(lambda subkey: jax.random.permutation(subkey, COL_LOC))(jax.random.split(key_place, colgroups))
    places = places.astype(jnp.int32)
    target = jnp.where(labels_all == 0, 0, jnp.where(labels_all == colgroups - 1, COL_LOC - 1, places[:, 0]))
    found = jnp.argmax((places == target[:, None]).astype(jnp.int32), axis=1).astype(jnp.int32)
    column = jnp.arange(COL_LOC, dtype=jnp.int32)[None, :]
    places = jnp.where(column == 0, target[:, None], jnp.where(column == found[:, None], places[:, 0:1], places))
    return (labels * COL_LOC + places[labels, rank]).astype(jnp.int32)


def draw_row_maps(key, part):
    first, second = jax.random.split(key)
    return jnp.stack([child_map(first), child_map(second)])


def shard_levels(key, extent, cuts, low, top_value):
    loudness, own = 1.0, jax.random.fold_in(key, 6)
    for dim, blocks in cuts:
        steps = jnp.exp(jax.random.uniform(jax.random.fold_in(own, dim), (blocks,), jnp.float32, low / len(cuts), top_value / len(cuts)))
        loudness = loudness * jnp.repeat(steps, extent[dim] // blocks).reshape([-1 if axis == dim else 1 for axis in range(len(extent))])
    return loudness


def gaussian(stream_key, extent, width, most, cuts=(), kind=jnp.bfloat16):
    entries = width * jax.random.normal(stream_key, extent, jnp.float32)
    if cuts:
        entries = entries * shard_levels(stream_key, extent, cuts, -0.22, 0.18)
    return jnp.clip(entries, -most, most).astype(kind)


def setup_inputs(seed: int = 0) -> dict:
    arg_keys = jax.random.split(jax.random.key(seed), 5)
    return {
        "parent_front": gaussian(arg_keys[0], (PARENT, PARENT), 1.0, 6.0, ((0, 16), (1, 16)), jnp.float32),
        "child_blocks": gaussian(arg_keys[1], (2, CHILD, CHILD), 1.0, 6.0, ((0, 2), (1, 8), (2, 16)), jnp.float32),
        "row_maps": draw_row_maps(jax.random.fold_in(arg_keys[4], 71), 0),
        "inverse_blocks": gaussian(arg_keys[3], (NPB, PB, PB), 0.02, 0.12, (), jnp.float32),
    }


def highest_dot(left, right):
    return jnp.dot(left, right, precision=lax.Precision.HIGHEST, preferred_element_type=jnp.float32)


def reference(parent_front, child_blocks, row_maps, inverse_blocks):
    assembled = parent_front
    for child in range(2):
        spread = jnp.zeros((CHILD, PARENT), jnp.float32).at[:, row_maps[child]].set(child_blocks[child])
        assembled = assembled.at[row_maps[child]].add(spread)
    factors = []
    for block in range(NPB):
        current = assembled[:, block * PB:(block + 1) * PB]
        if block > 0:
            earlier = jnp.concatenate(factors, axis=1)
            current = current - highest_dot(earlier, earlier[block * PB:(block + 1) * PB].T)
        factors.append(highest_dot(current, jnp.tril(inverse_blocks[block]).T))
    factor = jnp.concatenate(factors, axis=1)
    updated_front = assembled - highest_dot(factor, factor.T)
    return updated_front, factor.astype(jnp.bfloat16)
```

```python
import functools

import jax
import jax.numpy as jnp
from jax import lax
from jax.experimental import pallas as pl
from jax.experimental.pallas import tpu as pltpu
from jax.sharding import PartitionSpec as P

MESH = pl.DeviceIdType.MESH
F32 = jnp.float32
BF16 = jnp.bfloat16

SUB = 512
CAP = 64
LOC = 1024
GROUPS = 16
WIDTH = 128
BLOCKS = 4
PANEL = WIDTH * BLOCKS


def halves(value):
    high = lax.reduce_precision(value, 8, 7)
    return high.astype(BF16), (value - high).astype(BF16)


def dot(left, right, dims):
    return lax.dot_general(left, right, (dims, ((), ())), preferred_element_type=F32)


def before(flags):
    size = flags.shape[-1]
    upper = jnp.arange(size)[:, None] < jnp.arange(size)[None, :]
    return jnp.dot(flags.astype(BF16), upper.astype(BF16), preferred_element_type=F32).astype(jnp.int32)


def send_slots(parents):
    targets = parents // LOC
    member = targets[:, None, :] == jnp.arange(GROUPS, dtype=jnp.int32)[None, :, None]
    rank = jnp.sum(before(member) * member.astype(jnp.int32), axis=1)
    return targets, rank


def landing(parents, mine):
    member = parents // LOC == mine
    rank = jnp.where(member, before(member), -1)
    hit = rank[:, :, None, :] == jnp.arange(CAP, dtype=jnp.int32)[None, None, :, None]
    return jnp.sum(jnp.where(hit, (parents % LOC + 1)[:, :, None, :], 0), axis=-1) - 1


def place():
    half, row, col = lax.axis_index("half"), lax.axis_index("row"), lax.axis_index("col")
    return half, row // 4, row % 4, col // 4, col % 4


def device(half, z_hi, x, y, z_lo):
    return {"half": half, "row": z_hi * 4 + x, "col": y * 4 + z_lo}


def group_tree(half, z_hi, x, y, z_lo, src_half, src_z, src_x):
    away = (x - src_x + 4) % 4
    lead = half == src_half
    source = lead & (z_hi == src_z) & (away == 0)
    children = [
        (source, device(half, 1 - z_hi, x, y, z_lo)),
        (lead & (away <= 1), device(half, z_hi, (x + 1) % 4, y, z_lo)),
        (lead & (away == 0), device(half, z_hi, (x + 3) % 4, y, z_lo)),
        (lead, device(1 - half, z_hi, x, y, z_lo)),
    ]
    up_x = jnp.where(away == 3, (x + 1) % 4, (x + 3) % 4)
    parent_half = jnp.where(lead, half, 1 - half)
    parent_z = jnp.where(lead & (away == 0), 1 - z_hi, z_hi)
    parent_x = jnp.where(lead & (away != 0), up_x, x)
    parent = device(parent_half, parent_z, parent_x, y, z_lo)
    hops = jnp.where(away == 3, 1, away) + jnp.where(lead, 0, 1) + jnp.where(z_hi == src_z, 0, 2)
    return source, children, parent, hops


def z_first_tree(half, z_hi, x, y, z_lo):
    at = lambda y2, z2: device(half, z_hi, x, y2, z2)
    children = [
        ((y == 0) & (z_lo < 3), at(0, z_lo + 1)),
        ((y <= 1) & (z_lo >= 1), at(y + 1, z_lo)),
        ((y == 0) & (z_lo >= 1), at(3, z_lo)),
        ((y >= 1) & (z_lo == 1), at(y, 0)),
    ]
    back = (z_lo == 0) & (y >= 1)
    parent_y = jnp.where(back, y, jnp.where(y == 2, 1, 0))
    parent_z = jnp.where(back, 1, jnp.where(y == 0, z_lo - 1, z_lo))
    turn = jnp.where(y == 3, 1, y)
    hops = jnp.where(back, turn + 2, turn + z_lo)
    return children, at(parent_y, parent_z), hops


def y_first_tree(half, z_hi, x, y, z_lo):
    at = lambda y2, z2: device(half, z_hi, x, y2, z2)
    children = [
        ((z_lo == 0) & (y <= 1), at(y + 1, 0)),
        ((z_lo == 0) & (y == 0), at(3, 0)),
        ((y >= 1) & (z_lo < 3), at(y, z_lo + 1)),
        ((y == 1) & (z_lo >= 1), at(0, z_lo)),
    ]
    back = (y == 0) & (z_lo >= 1)
    parent_y = jnp.where(z_lo == 0, jnp.where(y == 2, 1, 0), jnp.where(y == 0, 1, y))
    parent_z = jnp.where((z_lo == 0) | back, z_lo, z_lo - 1)
    turn = jnp.where(y == 3, 1, y)
    hops = jnp.where(back, z_lo + 2, turn + z_lo)
    return children, at(parent_y, parent_z), hops


def count(children):
    total = 0
    for cond, _ in children:
        total = total + cond.astype(jnp.int32)
    return total


def wait_for(barrier, signals):
    @pl.when(signals > 0)
    def _():
        pl.semaphore_wait(barrier, signals)


def remote(src, dst, send, recv, target):
    return pltpu.make_async_remote_copy(
        src_ref=src, dst_ref=dst, send_sem=send, recv_sem=recv, device_id=target, device_id_type=MESH
    )


def split(value):
    high = value.astype(BF16)
    return high, (value - high.astype(F32)).astype(BF16)


def outer(left, right):
    left_high, left_low = split(left)
    right_high, right_low = split(right)
    dims = ((1,), (1,))
    return dot(left_high, right_high, dims) + (dot(left_high, right_low, dims) + dot(left_low, right_high, dims))


def panel_kernel(a_ref, inv_ref, f_ref, d_ref, l_ref, send, recv, own):
    half, z_hi, x, y, z_lo = place()
    source, children, parent, _ = group_tree(half, z_hi, x, y, z_lo, 0, 0, 0)
    active = (y == 0) & (z_lo == 0)
    barrier = pltpu.get_barrier_semaphore()

    @pl.when(active)
    def _():
        @pl.when(jnp.logical_not(source))
        def _():
            pl.semaphore_signal(barrier, inc=1, device_id=parent, device_id_type=MESH)

        wait_for(barrier, count(children))

        def piece(ref, block):
            return ref.at[pl.ds(block * WIDTH, WIDTH), pl.ds(0, block * WIDTH)]

        def copy(block, number):
            return remote(
                piece(d_ref, block), piece(d_ref, block), send.at[number, block - 1], recv.at[block - 1], children[number][1]
            )

        for block in range(1, BLOCKS):
            @pl.when(source)
            def _():
                mine = pltpu.make_async_copy(piece(a_ref, block), piece(d_ref, block), own)
                mine.start()
                mine.wait()

            @pl.when(jnp.logical_not(source))
            def _():
                copy(block, 0).wait_recv()

            for number, (cond, _) in enumerate(children):
                @pl.when(cond)
                def _():
                    copy(block, number).start()

        lower = lax.broadcasted_iota(jnp.int32, (WIDTH, WIDTH), 0) >= lax.broadcasted_iota(jnp.int32, (WIDTH, WIDTH), 1)
        for block in range(BLOCKS):
            inverse = jnp.where(lower, inv_ref[block], 0.0)
            here = pl.ds(block * WIDTH, WIDTH)
            done = pl.ds(0, block * WIDTH)
            current = a_ref[:, here]
            if block > 0:
                above = l_ref[here, done]
                current = current - outer(f_ref[:, done], above)
            f_ref[:, here] = outer(current, inverse)
            if block + 1 < BLOCKS:
                below = pl.ds((block + 1) * WIDTH, PANEL - (block + 1) * WIDTH)
                current = d_ref[below, here]
                if block > 0:
                    current = current - outer(l_ref[below, done], above)
                l_ref[below, here] = outer(current, inverse)

        for block in range(1, BLOCKS):
            for number, (cond, _) in enumerate(children):
                @pl.when(cond)
                def _():
                    copy(block, number).wait_send()


def panel(a, inverse_blocks):
    return pl.pallas_call(
        panel_kernel,
        out_shape=jax.ShapeDtypeStruct(a.shape, F32),
        in_specs=[pl.BlockSpec(memory_space=pltpu.VMEM)] * 2,
        out_specs=pl.BlockSpec(memory_space=pltpu.VMEM),
        scratch_shapes=[
            pltpu.VMEM((PANEL, PANEL), F32),
            pltpu.VMEM((PANEL, PANEL), F32),
            pltpu.SemaphoreType.DMA((4, BLOCKS - 1)),
            pltpu.SemaphoreType.DMA((BLOCKS - 1,)),
            pltpu.SemaphoreType.DMA,
        ],
        compiler_params=pltpu.CompilerParams(collective_id=0, has_side_effects=True, vmem_limit_bytes=24 * 2**20),
        name="panel",
    )(a, inverse_blocks)


CHUNK = 32
STEP = 2


def spread_kernel(f_ref, row_ref, col_ref, recv_z, recv_y, recv_g, send_z, send_y, send_g, own):
    half, z_hi, x, y, z_lo = place()
    side = row_ref.shape[0] // 2
    chunks = side // CHUNK
    tree_z, parent_z, hops_z = z_first_tree(half, z_hi, x, y, z_lo)
    tree_y, parent_y, hops_y = y_first_tree(half, z_hi, x, y, z_lo)
    source, tree_g, parent_g, hops_g = group_tree(half, z_hi, x, y, z_lo, y // 2, y % 2, z_lo)
    root = (y == 0) & (z_lo == 0)
    barrier = pltpu.get_barrier_semaphore()

    @pl.when(jnp.logical_not(root))
    def _():
        pl.semaphore_signal(barrier, inc=1, device_id=parent_z, device_id_type=MESH)
        pl.semaphore_signal(barrier, inc=1, device_id=parent_y, device_id_type=MESH)

    @pl.when(jnp.logical_not(source))
    def _():
        pl.semaphore_signal(barrier, inc=1, device_id=parent_g, device_id_type=MESH)

    @pl.when(root)
    def _():
        mine = pltpu.make_async_copy(f_ref, row_ref, own)
        mine.start()
        mine.wait()

    wait_for(barrier, count(tree_z) + count(tree_y) + count(tree_g))

    def rows(number):
        return pl.ds(pl.multiple_of(number * CHUNK, CHUNK), CHUNK)

    def forward(src, dst, number, tree, sends, recv):
        for slot, (cond, target) in enumerate(tree):
            @pl.when(cond)
            def _():
                remote(src.at[rows(number)], dst.at[rows(number)], sends.at[slot], recv, target).start()

    def along_row(number, offset, tree, sends, recv):
        @pl.when((number >= 0) & (number < chunks))
        def _():
            @pl.when(jnp.logical_not(root))
            def _():
                at = row_ref.at[rows(offset + number)]
                remote(at, at, sends.at[0], recv.at[number], tree[0][1]).wait_recv()

            forward(row_ref, row_ref, offset + number, tree, sends, recv.at[number])

            @pl.when(source)
            def _():
                forward(row_ref, col_ref, offset + number, tree_g, send_g, recv_g.at[offset + number])

    def along_col(number, offset):
        @pl.when((number >= 0) & (number < chunks) & jnp.logical_not(source))
        def _():
            at = col_ref.at[rows(offset + number)]
            remote(at, at, send_g.at[0], recv_g.at[offset + number], tree_g[0][1]).wait_recv()
            forward(col_ref, col_ref, offset + number, tree_g, send_g, recv_g.at[offset + number])

    start_z, start_y, start_g = hops_z * STEP, hops_y * STEP, hops_g * STEP

    def body(step, carry):
        along_row(step - start_z, 0, tree_z, send_z, recv_z)
        along_row(step - start_y, chunks, tree_y, send_y, recv_y)
        along_col(step - start_z - start_g, 0)
        along_col(step - start_y - start_g, chunks)
        return carry

    lax.fori_loop(0, chunks + STEP * 11, body, 0)

    @pl.when(source)
    def _():
        mine = pltpu.make_async_copy(row_ref, col_ref, own)
        mine.start()
        mine.wait()

    def drain(tree, sends, size):
        at = row_ref.at[pl.ds(0, size)]
        for slot, (cond, target) in enumerate(tree):
            @pl.when(cond)
            def _():
                remote(at, at, sends.at[slot], recv_z.at[0], target).wait_send()

    drain(tree_z, send_z, side)
    drain(tree_y, send_y, side)
    drain(tree_g, send_g, 2 * side)


def spread(f):
    chunks = f.shape[0] // 2 // CHUNK
    return pl.pallas_call(
        spread_kernel,
        out_shape=[jax.ShapeDtypeStruct(f.shape, F32)] * 2,
        in_specs=[pl.BlockSpec(memory_space=pltpu.VMEM)],
        out_specs=[pl.BlockSpec(memory_space=pltpu.VMEM)] * 2,
        scratch_shapes=[
            pltpu.SemaphoreType.DMA((chunks,)),
            pltpu.SemaphoreType.DMA((chunks,)),
            pltpu.SemaphoreType.DMA((2 * chunks,)),
            pltpu.SemaphoreType.DMA((4,)),
            pltpu.SemaphoreType.DMA((4,)),
            pltpu.SemaphoreType.DMA((4,)),
            pltpu.SemaphoreType.DMA,
        ],
        compiler_params=pltpu.CompilerParams(collective_id=1, has_side_effects=True, vmem_limit_bytes=24 * 2**20),
        name="spread",
    )(f)


def local(parent_front, child_blocks, row_maps, inverse_blocks):
    half, row, col = lax.axis_index("half"), lax.axis_index("row"), lax.axis_index("col")
    group = half * 8 + row
    maps = row_maps.reshape(2, -1, SUB)

    mine = lax.dynamic_index_in_dim(maps, half, 0, keepdims=False)
    row_target, row_rank = send_slots(lax.dynamic_slice_in_dim(mine, 2 * row, 2, 0))
    row_slot = (row_target * 2 + jnp.arange(2, dtype=jnp.int32)[:, None]) * CAP + row_rank
    col_target, col_rank = send_slots(lax.dynamic_slice_in_dim(mine, col, 1, 0))
    col_slot = (col_target * CAP + col_rank).reshape(-1)
    row_pick = (row_slot.reshape(-1)[:, None] == jnp.arange(GROUPS * 2 * CAP, dtype=jnp.int32)).astype(BF16)
    col_pick = (jnp.arange(GROUPS * CAP, dtype=jnp.int32)[:, None] == col_slot).astype(BF16)
    packed = 0
    for part in halves(child_blocks[0]):
        by_col = dot(col_pick, part, ((1,), (1,))).astype(BF16)
        packed = packed + dot(by_col, row_pick, ((1,), (0,)))
    packed = packed.reshape(GROUPS, CAP, GROUPS, 2 * CAP).transpose(2, 0, 1, 3)

    moved = lax.all_to_all(
        packed.reshape(GROUPS * GROUPS * CAP, 2 * CAP), ("half", "row", "col"), split_axis=0, concat_axis=0, tiled=True
    ).reshape(GROUPS, GROUPS, CAP, 2 * CAP)

    row_land = landing(maps, group).reshape(-1)
    col_land = landing(maps, col).reshape(2, -1)
    places = jnp.arange(LOC, dtype=jnp.int32)
    row_put = (places[:, None] == row_land).astype(BF16)
    col_put = (col_land[:, :, None] == places).astype(BF16)
    assembled = parent_front
    for part in halves(moved.transpose(0, 1, 2, 3).reshape(2, 8, GROUPS * CAP, 2 * CAP)):
        by_row = jnp.einsum("ksqr,kqp->ksrp", part, col_put, preferred_element_type=F32).astype(BF16)
        assembled = assembled + dot(row_put, by_row.reshape(-1, LOC), ((1,), (0,)))

    factor = panel(assembled[:, :PANEL], inverse_blocks)
    factor_rows, factor_cols = spread(factor)
    product = lax.dot_general(
        factor_rows, factor_cols, (((1,), (1,)), ((), ())), precision=lax.Precision.HIGH, preferred_element_type=F32
    )
    return assembled - product, factor_rows.astype(BF16)


def solution(mesh):
    in_specs = (P(("half", "row"), "col"), P("half", "row", "col"), P(), P())
    out_specs = (P(("half", "row"), "col"), P(("half", "row"), None))
    return jax.shard_map(local, mesh=mesh, in_specs=in_specs, out_specs=out_specs, check_vma=False)
```

```python
import functools

import jax
import jax.numpy as jnp
from jax import lax
from jax.experimental import pallas as pl
from jax.experimental.pallas import tpu as pltpu
from jax.sharding import PartitionSpec as P

MESH = pl.DeviceIdType.MESH
F32 = jnp.float32
BF16 = jnp.bfloat16

SUB = 512
CAP = 64
LOC = 1024
GROUPS = 16
WIDTH = 128
BLOCKS = 4
PANEL = WIDTH * BLOCKS


def dot(left, right, dims):
    return lax.dot_general(left, right, (dims, ((), ())), preferred_element_type=F32)


def before(flags):
    size = flags.shape[-1]
    upper = jnp.arange(size)[:, None] < jnp.arange(size)[None, :]
    return jnp.dot(flags.astype(BF16), upper.astype(BF16), preferred_element_type=F32).astype(jnp.int32)


def send_slots(parents):
    targets = parents // LOC
    member = targets[:, None, :] == jnp.arange(GROUPS, dtype=jnp.int32)[None, :, None]
    rank = jnp.sum(before(member) * member.astype(jnp.int32), axis=1)
    return targets, rank


def landing(parents, mine):
    member = parents // LOC == mine
    rank = jnp.where(member, before(member), -1)
    hit = rank[:, :, None, :] == jnp.arange(CAP, dtype=jnp.int32)[None, None, :, None]
    return jnp.sum(jnp.where(hit, (parents % LOC + 1)[:, :, None, :], 0), axis=-1) - 1


def place():
    half, row, col = lax.axis_index("half"), lax.axis_index("row"), lax.axis_index("col")
    return half, row // 4, row % 4, col // 4, col % 4


def device(half, z_hi, x, y, z_lo):
    return {"half": half, "row": z_hi * 4 + x, "col": y * 4 + z_lo}


def group_tree(half, z_hi, x, y, z_lo, src_half, src_z, src_x):
    away = (x - src_x + 4) % 4
    lead = half == src_half
    source = lead & (z_hi == src_z) & (away == 0)
    children = [
        (source, device(half, 1 - z_hi, x, y, z_lo)),
        (lead & (away <= 1), device(half, z_hi, (x + 1) % 4, y, z_lo)),
        (lead & (away == 0), device(half, z_hi, (x + 3) % 4, y, z_lo)),
        (lead, device(1 - half, z_hi, x, y, z_lo)),
    ]
    up_x = jnp.where(away == 3, (x + 1) % 4, (x + 3) % 4)
    parent_half = jnp.where(lead, half, 1 - half)
    parent_z = jnp.where(lead & (away == 0), 1 - z_hi, z_hi)
    parent_x = jnp.where(lead & (away != 0), up_x, x)
    parent = device(parent_half, parent_z, parent_x, y, z_lo)
    hops = jnp.where(away == 3, 1, away) + jnp.where(lead, 0, 1) + jnp.where(z_hi == src_z, 0, 2)
    return source, children, parent, hops


def z_first_tree(half, z_hi, x, y, z_lo):
    at = lambda y2, z2: device(half, z_hi, x, y2, z2)
    children = [
        ((y == 0) & (z_lo < 3), at(0, z_lo + 1)),
        ((y <= 1) & (z_lo >= 1), at(y + 1, z_lo)),
        ((y == 0) & (z_lo >= 1), at(3, z_lo)),
        ((y >= 1) & (z_lo == 1), at(y, 0)),
    ]
    back = (z_lo == 0) & (y >= 1)
    parent_y = jnp.where(back, y, jnp.where(y == 2, 1, 0))
    parent_z = jnp.where(back, 1, jnp.where(y == 0, z_lo - 1, z_lo))
    turn = jnp.where(y == 3, 1, y)
    hops = jnp.where(back, turn + 2, turn + z_lo)
    return children, at(parent_y, parent_z), hops


def y_first_tree(half, z_hi, x, y, z_lo):
    at = lambda y2, z2: device(half, z_hi, x, y2, z2)
    children = [
        ((z_lo == 0) & (y <= 1), at(y + 1, 0)),
        ((z_lo == 0) & (y == 0), at(3, 0)),
        ((y >= 1) & (z_lo < 3), at(y, z_lo + 1)),
        ((y == 1) & (z_lo >= 1), at(0, z_lo)),
    ]
    back = (y == 0) & (z_lo >= 1)
    parent_y = jnp.where(z_lo == 0, jnp.where(y == 2, 1, 0), jnp.where(y == 0, 1, y))
    parent_z = jnp.where((z_lo == 0) | back, z_lo, z_lo - 1)
    turn = jnp.where(y == 3, 1, y)
    hops = jnp.where(back, z_lo + 2, turn + z_lo)
    return children, at(parent_y, parent_z), hops


def count(children):
    total = 0
    for cond, _ in children:
        total = total + cond.astype(jnp.int32)
    return total


def wait_for(barrier, signals):
    @pl.when(signals > 0)
    def _():
        pl.semaphore_wait(barrier, signals)


def remote(src, dst, send, recv, target):
    return pltpu.make_async_remote_copy(
        src_ref=src, dst_ref=dst, send_sem=send, recv_sem=recv, device_id=target, device_id_type=MESH
    )


def split(value):
    high = value.astype(BF16)
    return high, (value - high.astype(F32)).astype(BF16)


def outer(left, right):
    left_high, left_low = split(left)
    right_high, right_low = split(right)
    dims = ((1,), (1,))
    return dot(left_high, right_high, dims) + (dot(left_high, right_low, dims) + dot(left_low, right_high, dims))


def panel_kernel(a_ref, inv_ref, f_ref, d_ref, l_ref, send, recv, own):
    half, z_hi, x, y, z_lo = place()
    source, children, parent, _ = group_tree(half, z_hi, x, y, z_lo, 0, 0, 0)
    active = (y == 0) & (z_lo == 0)
    barrier = pltpu.get_barrier_semaphore()

    @pl.when(active)
    def _():
        @pl.when(jnp.logical_not(source))
        def _():
            pl.semaphore_signal(barrier, inc=1, device_id=parent, device_id_type=MESH)

        wait_for(barrier, count(children))

        def piece(ref, block):
            return ref.at[pl.ds(block * WIDTH, WIDTH), pl.ds(0, block * WIDTH)]

        def copy(block, number):
            return remote(
                piece(d_ref, block), piece(d_ref, block), send.at[number, block - 1], recv.at[block - 1], children[number][1]
            )

        for block in range(1, BLOCKS):
            @pl.when(source)
            def _():
                mine = pltpu.make_async_copy(piece(a_ref, block), piece(d_ref, block), own)
                mine.start()
                mine.wait()

            @pl.when(jnp.logical_not(source))
            def _():
                copy(block, 0).wait_recv()

            for number, (cond, _) in enumerate(children):
                @pl.when(cond)
                def _():
                    copy(block, number).start()

        lower = lax.broadcasted_iota(jnp.int32, (WIDTH, WIDTH), 0) >= lax.broadcasted_iota(jnp.int32, (WIDTH, WIDTH), 1)
        for block in range(BLOCKS):
            inverse = jnp.where(lower, inv_ref[block], 0.0)
            here = pl.ds(block * WIDTH, WIDTH)
            done = pl.ds(0, block * WIDTH)
            current = a_ref[:, here]
            if block > 0:
                above = l_ref[here, done]
                current = current - outer(f_ref[:, done], above)
            f_ref[:, here] = outer(current, inverse)
            if block + 1 < BLOCKS:
                below = pl.ds((block + 1) * WIDTH, PANEL - (block + 1) * WIDTH)
                current = d_ref[below, here]
                if block > 0:
                    current = current - outer(l_ref[below, done], above)
                l_ref[below, here] = outer(current, inverse)

        for block in range(1, BLOCKS):
            for number, (cond, _) in enumerate(children):
                @pl.when(cond)
                def _():
                    copy(block, number).wait_send()


def panel(a, inverse_blocks):
    return pl.pallas_call(
        panel_kernel,
        out_shape=jax.ShapeDtypeStruct(a.shape, F32),
        in_specs=[pl.BlockSpec(memory_space=pltpu.VMEM)] * 2,
        out_specs=pl.BlockSpec(memory_space=pltpu.VMEM),
        scratch_shapes=[
            pltpu.VMEM((PANEL, PANEL), F32),
            pltpu.VMEM((PANEL, PANEL), F32),
            pltpu.SemaphoreType.DMA((4, BLOCKS - 1)),
            pltpu.SemaphoreType.DMA((BLOCKS - 1,)),
            pltpu.SemaphoreType.DMA,
        ],
        compiler_params=pltpu.CompilerParams(collective_id=0, has_side_effects=True, vmem_limit_bytes=24 * 2**20),
        name="panel",
    )(a, inverse_blocks)


CHUNK = 32
STEP = 2


def spread_kernel(f_ref, row_ref, col_ref, recv_z, recv_y, recv_g, send_z, send_y, send_g, own):
    half, z_hi, x, y, z_lo = place()
    side = row_ref.shape[0] // 2
    chunks = side // CHUNK
    tree_z, parent_z, hops_z = z_first_tree(half, z_hi, x, y, z_lo)
    tree_y, parent_y, hops_y = y_first_tree(half, z_hi, x, y, z_lo)
    source, tree_g, parent_g, hops_g = group_tree(half, z_hi, x, y, z_lo, y // 2, y % 2, z_lo)
    root = (y == 0) & (z_lo == 0)
    barrier = pltpu.get_barrier_semaphore()

    @pl.when(jnp.logical_not(root))
    def _():
        pl.semaphore_signal(barrier, inc=1, device_id=parent_z, device_id_type=MESH)
        pl.semaphore_signal(barrier, inc=1, device_id=parent_y, device_id_type=MESH)

    @pl.when(jnp.logical_not(source))
    def _():
        pl.semaphore_signal(barrier, inc=1, device_id=parent_g, device_id_type=MESH)

    @pl.when(root)
    def _():
        mine = pltpu.make_async_copy(f_ref, row_ref, own)
        mine.start()
        mine.wait()

    wait_for(barrier, count(tree_z) + count(tree_y) + count(tree_g))

    def rows(number):
        return pl.ds(pl.multiple_of(number * CHUNK, CHUNK), CHUNK)

    def forward(src, dst, number, tree, sends, recv):
        for slot, (cond, target) in enumerate(tree):
            @pl.when(cond)
            def _():
                remote(src.at[rows(number)], dst.at[rows(number)], sends.at[slot], recv, target).start()

    def along_row(number, offset, tree, sends, recv):
        @pl.when((number >= 0) & (number < chunks))
        def _():
            @pl.when(jnp.logical_not(root))
            def _():
                at = row_ref.at[rows(offset + number)]
                remote(at, at, sends.at[0], recv.at[number], tree[0][1]).wait_recv()

            forward(row_ref, row_ref, offset + number, tree, sends, recv.at[number])

            @pl.when(source)
            def _():
                forward(row_ref, col_ref, offset + number, tree_g, send_g, recv_g.at[offset + number])

    def along_col(number, offset):
        @pl.when((number >= 0) & (number < chunks) & jnp.logical_not(source))
        def _():
            at = col_ref.at[rows(offset + number)]
            remote(at, at, send_g.at[0], recv_g.at[offset + number], tree_g[0][1]).wait_recv()
            forward(col_ref, col_ref, offset + number, tree_g, send_g, recv_g.at[offset + number])

    start_z, start_y, start_g = hops_z * STEP, hops_y * STEP, hops_g * STEP

    def body(step, carry):
        along_row(step - start_z, 0, tree_z, send_z, recv_z)
        along_row(step - start_y, chunks, tree_y, send_y, recv_y)
        along_col(step - start_z - start_g, 0)
        along_col(step - start_y - start_g, chunks)
        return carry

    lax.fori_loop(0, chunks + STEP * 11, body, 0)

    @pl.when(source)
    def _():
        mine = pltpu.make_async_copy(row_ref, col_ref, own)
        mine.start()
        mine.wait()

    def drain(tree, sends, size):
        at = row_ref.at[pl.ds(0, size)]
        for slot, (cond, target) in enumerate(tree):
            @pl.when(cond)
            def _():
                remote(at, at, sends.at[slot], recv_z.at[0], target).wait_send()

    drain(tree_z, send_z, side)
    drain(tree_y, send_y, side)
    drain(tree_g, send_g, 2 * side)


def spread(f):
    chunks = f.shape[0] // 2 // CHUNK
    return pl.pallas_call(
        spread_kernel,
        out_shape=[jax.ShapeDtypeStruct(f.shape, F32)] * 2,
        in_specs=[pl.BlockSpec(memory_space=pltpu.VMEM)],
        out_specs=[pl.BlockSpec(memory_space=pltpu.VMEM)] * 2,
        scratch_shapes=[
            pltpu.SemaphoreType.DMA((chunks,)),
            pltpu.SemaphoreType.DMA((chunks,)),
            pltpu.SemaphoreType.DMA((2 * chunks,)),
            pltpu.SemaphoreType.DMA((4,)),
            pltpu.SemaphoreType.DMA((4,)),
            pltpu.SemaphoreType.DMA((4,)),
            pltpu.SemaphoreType.DMA,
        ],
        compiler_params=pltpu.CompilerParams(collective_id=1, has_side_effects=True, vmem_limit_bytes=24 * 2**20),
        name="spread",
    )(f)


def exchange_kernel(
    x_ref, parent_ref, row_ref, col_ref, row_land_ref, col_land_ref, out_ref,
    held, packed, landed, pick, by_col, parts, by_row, put,
    own, first, ring_sent, ring_got, sent, got, kept,
):
    half, z_hi, x, y, z_lo = place()
    z = z_hi * 4 + z_lo
    mid = held.shape[1] // 2
    tile = 256
    rows_dims = ((1,), (1,))
    up, down = (z + 1) % 8, (z + 7) % 8
    above = device(half, up // 4, x, y, up % 4)
    below = device(half, down // 4, x, y, down % 4)

    def peer(number):
        return device((half + number // 16) % 2, z_hi, (x + number // 4) % 4, (y + number) % 4, z_lo)

    mine = pltpu.make_async_copy(x_ref, held.at[0], own)
    mine.start()
    front = pltpu.make_async_copy(parent_ref, out_ref, first)
    front.start()
    barrier = pltpu.get_barrier_semaphore()
    for target in (above, below):
        pl.semaphore_signal(barrier, inc=1, device_id=target, device_id_type=MESH)

    def greet(number, carry):
        pl.semaphore_signal(barrier, inc=1, device_id=peer(number), device_id_type=MESH)
        return carry

    lax.fori_loop(1, 32, greet, 0)
    mine.wait()
    pl.semaphore_wait(barrier, 33)

    def at_of(number):
        return jnp.where(number % 2 == 1, 8 - (number + 1) // 2, number // 2)

    def part(at, side):
        return held.at[at, pl.ds(side * mid, mid), :]

    def ring(at, side, way):
        to = (at + 7) % 8 if way == 0 else (at + 1) % 8
        return remote(
            part(at, side), part(to, side), ring_sent.at[way, at, side], ring_got.at[to, side], (above, below)[way]
        )

    def arrived(at, side):
        remote(part(at, side), part(at, side), ring_sent.at[0, at, side], ring_got.at[at, side], above).wait_recv()

    def message(number, to):
        to_half, to_x, to_y = (half + to // 16) % 2, (x + to // 4) % 4, (y + to) % 4
        src = packed.at[
            number % 4,
            pl.ds(pl.multiple_of(to_y * CAP, CAP), CAP),
            pl.ds(pl.multiple_of((to_half * 4 + to_x) * 128, 128), 128),
        ]
        dst = landed.at[
            at_of(number), half, pl.ds(pl.multiple_of(y * CAP, CAP), CAP), pl.ds(pl.multiple_of(x * 128, 128), 128)
        ]
        return src, dst

    def deliver(number):
        src, dst = message(number, 0)
        pltpu.make_async_copy(src, dst, kept.at[number]).start()

        def one(to, carry):
            src, dst = message(number, to)
            remote(src, dst, sent.at[number], got.at[number], peer(to)).start()
            return carry

        lax.fori_loop(1, 32, one, 0)

    def others():
        return out_ref.at[pl.ds(0, 31 * 8), :]

    def gone(number):
        remote(others(), others(), sent.at[number], got.at[number], above).wait_send()

    def landed_all(number):
        remote(others(), others(), sent.at[number], got.at[number], above).wait_recv()
        src, dst = message(number, 0)
        pltpu.make_async_copy(src, dst, kept.at[number]).wait()

    def pack(number):
        at = at_of(number)
        there = (z + at) % 8
        slots = lax.broadcasted_iota(jnp.int32, (4 * CAP, SUB), 0)
        col_pick = (slots == col_ref[there % 4]).astype(F32).astype(BF16)

        def columns(step, carry):
            here = pl.ds(pl.multiple_of(step * tile, tile), tile)
            high, low = split(held[at, here, :])
            by_col[: 4 * CAP, here] = dot(col_pick, high, rows_dims).astype(BF16)
            by_col[4 * CAP :, here] = dot(col_pick, low, rows_dims).astype(BF16)
            return carry

        lax.fori_loop(0, LOC // tile, columns, 0)

        def rows(step, carry):
            here = pl.ds(pl.multiple_of(step * tile, tile), tile)
            both = dot(by_col[...], pick[there // 4, here, :], rows_dims)
            packed[number % 4, :, here] = both[: 4 * CAP] + both[4 * CAP :]
            return carry

        lax.fori_loop(0, LOC // tile, rows, 0)

    def rows_of(number, child, step):
        source = (z + at_of(number)) % 8 // 4
        places = lax.broadcasted_iota(jnp.int32, (tile, SUB), 0) + step * tile
        row_put = (places == row_land_ref[child, source]).astype(F32).astype(BF16)
        return dot(row_put, parts[child], rows_dims).astype(BF16)

    def take(number):
        landed_all(number)
        for child in range(2):
            high, low = split(landed[at_of(number), child])
            parts[child, : 4 * CAP] = high
            parts[child, 4 * CAP :] = low

    def unpack_first(number):
        take(number)

        def rows(step, carry):
            here = pl.ds(pl.multiple_of(step * tile, tile), tile)
            for child in range(2):
                by_row[at_of(number) % 4, child, here, :] = rows_of(number, child, step)
            return carry

        lax.fori_loop(0, LOC // tile, rows, 0)

    def unpack_second(number, carry):
        source = (z + at_of(number)) % 4
        for child in range(2):
            places = lax.broadcasted_iota(jnp.int32, (LOC, 4 * CAP), 0)
            col_put = (places == col_land_ref[child, source]).astype(F32).astype(BF16)
            put[child, :, : 4 * CAP] = col_put
            put[child, :, 4 * CAP :] = col_put
        take(number)

        def rows(step, carry):
            here = pl.ds(pl.multiple_of(step * tile, tile), tile)
            total = out_ref[here, :]
            for child in range(2):
                both = by_row[at_of(number) % 4, child, here, :] + rows_of(number, child, step)
                total = total + dot(both, put[child], rows_dims)
            out_ref[here, :] = total
            return carry

        lax.fori_loop(0, LOC // tile, rows, 0)
        return carry

    for side in range(2):
        for way in range(2):
            ring(0, side, way).start()
    for source in range(2):
        slots = lax.broadcasted_iota(jnp.int32, pick.shape[1:], 0)
        pick[source] = (slots == row_ref[source]).astype(F32).astype(BF16)
    front.wait()

    def event(number, carry):
        @pl.when(number % 2 == 1)
        def _():
            step = (number + 1) // 2
            for side in range(2):
                arrived(8 - step, side)

                @pl.when(step < 4 - side)
                def _():
                    ring(8 - step, side, 0).start()

                @pl.when(step < 4)
                def _():
                    arrived(step, side)

                    @pl.when(step < 3 + side)
                    def _():
                        ring(step, side, 1).start()

        @pl.when(number >= 4)
        def _():
            gone(number - 4)

        pack(number)

        @pl.when((number >= 3) & (number < 7))
        def _():
            unpack_first(number - 3)

        deliver(number)
        return carry

    lax.fori_loop(0, 8, event, 0)
    lax.fori_loop(4, 8, unpack_second, 0)

    def settle(number, carry):
        gone(number)
        return carry

    lax.fori_loop(4, 8, settle, 0)
    for side in range(2):
        for at in (0, 7, 6, 5)[: 4 - side]:
            ring(at, side, 0).wait_send()
        for at in (0, 1, 2, 3)[: 3 + side]:
            ring(at, side, 1).wait_send()


def exchange(block, parent, row_slots, col_slots, row_land, col_land):
    rows, cols = block.shape
    return pl.pallas_call(
        exchange_kernel,
        out_shape=jax.ShapeDtypeStruct(parent.shape, F32),
        in_specs=[pl.BlockSpec(memory_space=pl.ANY)] * 2 + [pl.BlockSpec(memory_space=pltpu.VMEM)] * 4,
        out_specs=pl.BlockSpec(memory_space=pltpu.VMEM),
        scratch_shapes=[
            pltpu.VMEM((8, rows, cols), F32),
            pltpu.VMEM((4, 4 * CAP, LOC), F32),
            pltpu.VMEM((8, 2, 4 * CAP, SUB), F32),
            pltpu.VMEM((2, LOC, rows), BF16),
            pltpu.VMEM((8 * CAP, LOC), BF16),
            pltpu.VMEM((2, 8 * CAP, SUB), BF16),
            pltpu.VMEM((4, 2, LOC, 8 * CAP), BF16),
            pltpu.VMEM((2, LOC, 8 * CAP), BF16),
            pltpu.SemaphoreType.DMA,
            pltpu.SemaphoreType.DMA,
            pltpu.SemaphoreType.DMA((2, 8, 2)),
            pltpu.SemaphoreType.DMA((8, 2)),
            pltpu.SemaphoreType.DMA((8,)),
            pltpu.SemaphoreType.DMA((8,)),
            pltpu.SemaphoreType.DMA((8,)),
        ],
        compiler_params=pltpu.CompilerParams(collective_id=2, has_side_effects=True, vmem_limit_bytes=63 * 2**20),
        name="exchange",
    )(block, parent, row_slots, col_slots, row_land, col_land)


def local(parent_front, child_blocks, row_maps, inverse_blocks):
    half, row, col = lax.axis_index("half"), lax.axis_index("row"), lax.axis_index("col")
    group = half * 8 + row
    maps = row_maps.reshape(2, -1, SUB)

    mine = lax.dynamic_index_in_dim(maps, half, 0, keepdims=False)
    shards = mine.reshape(2, 4, 2 * SUB)
    target, rank = send_slots(lax.dynamic_index_in_dim(shards, row % 4, 1, keepdims=False).reshape(4, SUB))
    target, rank = target.reshape(2, 2, SUB), rank.reshape(2, 2, SUB)
    side = jnp.arange(2, dtype=jnp.int32)[:, None]
    slot = (((target // 8) * 4 + target % 4) * 2 + side) * CAP + rank
    row_slots = jnp.where(target // 4 % 2 == row // 4, slot, -1).reshape(2, 1, 2 * SUB)
    target, rank = send_slots(lax.dynamic_index_in_dim(mine.reshape(4, 4, SUB), col // 4, 0, keepdims=False))
    col_slots = jnp.where(target % 4 == col % 4, (target // 4) * CAP + rank, -1).reshape(4, 1, SUB)

    row_land = landing(maps, group).reshape(2, 2, 1, SUB)
    col_land = landing(maps, col).reshape(2, 4, 4, CAP).transpose(0, 2, 1, 3).reshape(2, 4, 1, 4 * CAP)
    assembled = exchange(child_blocks[0], parent_front, row_slots, col_slots, row_land, col_land)

    factor = panel(assembled[:, :PANEL], inverse_blocks)
    factor_rows, factor_cols = spread(factor)
    product = lax.dot_general(
        factor_rows, factor_cols, (((1,), (1,)), ((), ())), precision=lax.Precision.HIGH, preferred_element_type=F32
    )
    return assembled - product, factor_rows.astype(BF16)


def solution(mesh):
    in_specs = (P(("half", "row"), "col"), P("half", "row", "col"), P(), P())
    out_specs = (P(("half", "row"), "col"), P(("half", "row"), None))
    return jax.shard_map(local, mesh=mesh, in_specs=in_specs, out_specs=out_specs, check_vma=False)
```

```python
import functools

import jax
import jax.numpy as jnp
from jax import lax
from jax.experimental import pallas as pl
from jax.experimental.pallas import tpu as pltpu
from jax.sharding import PartitionSpec as P

MESH = pl.DeviceIdType.MESH
F32 = jnp.float32
BF16 = jnp.bfloat16

SUB = 512
CAP = 64
LOC = 1024
GROUPS = 16
WIDTH = 128
BLOCKS = 4
PANEL = WIDTH * BLOCKS


def dot(left, right, dims):
    return lax.dot_general(left, right, (dims, ((), ())), preferred_element_type=F32)


def before(flags):
    size = flags.shape[-1]
    upper = jnp.arange(size)[:, None] < jnp.arange(size)[None, :]
    return jnp.dot(flags.astype(BF16), upper.astype(BF16), preferred_element_type=F32).astype(jnp.int32)


def send_slots(parents):
    targets = parents // LOC
    member = targets[:, None, :] == jnp.arange(GROUPS, dtype=jnp.int32)[None, :, None]
    rank = jnp.sum(before(member) * member.astype(jnp.int32), axis=1)
    return targets, rank


def landing(parents, mine):
    member = parents // LOC == mine
    rank = jnp.where(member, before(member), -1)
    hit = rank[:, :, None, :] == jnp.arange(CAP, dtype=jnp.int32)[None, None, :, None]
    return jnp.sum(jnp.where(hit, (parents % LOC + 1)[:, :, None, :], 0), axis=-1) - 1


def place():
    half, row, col = lax.axis_index("half"), lax.axis_index("row"), lax.axis_index("col")
    return half, row // 4, row % 4, col // 4, col % 4


def device(half, z_hi, x, y, z_lo):
    return {"half": half, "row": z_hi * 4 + x, "col": y * 4 + z_lo}


def group_tree(half, z_hi, x, y, z_lo, src_half, src_z, src_x):
    away = (x - src_x + 4) % 4
    lead = half == src_half
    source = lead & (z_hi == src_z) & (away == 0)
    children = [
        (source, device(half, 1 - z_hi, x, y, z_lo)),
        (lead & (away <= 1), device(half, z_hi, (x + 1) % 4, y, z_lo)),
        (lead & (away == 0), device(half, z_hi, (x + 3) % 4, y, z_lo)),
        (lead, device(1 - half, z_hi, x, y, z_lo)),
    ]
    up_x = jnp.where(away == 3, (x + 1) % 4, (x + 3) % 4)
    parent_half = jnp.where(lead, half, 1 - half)
    parent_z = jnp.where(lead & (away == 0), 1 - z_hi, z_hi)
    parent_x = jnp.where(lead & (away != 0), up_x, x)
    parent = device(parent_half, parent_z, parent_x, y, z_lo)
    hops = jnp.where(away == 3, 1, away) + jnp.where(lead, 0, 1) + jnp.where(z_hi == src_z, 0, 2)
    return source, children, parent, hops


def z_first_tree(half, z_hi, x, y, z_lo):
    at = lambda y2, z2: device(half, z_hi, x, y2, z2)
    children = [
        ((y == 0) & (z_lo < 3), at(0, z_lo + 1)),
        ((y <= 1) & (z_lo >= 1), at(y + 1, z_lo)),
        ((y == 0) & (z_lo >= 1), at(3, z_lo)),
        ((y >= 1) & (z_lo == 1), at(y, 0)),
    ]
    back = (z_lo == 0) & (y >= 1)
    parent_y = jnp.where(back, y, jnp.where(y == 2, 1, 0))
    parent_z = jnp.where(back, 1, jnp.where(y == 0, z_lo - 1, z_lo))
    turn = jnp.where(y == 3, 1, y)
    hops = jnp.where(back, turn + 2, turn + z_lo)
    return children, at(parent_y, parent_z), hops


def y_first_tree(half, z_hi, x, y, z_lo):
    at = lambda y2, z2: device(half, z_hi, x, y2, z2)
    children = [
        ((z_lo == 0) & (y <= 1), at(y + 1, 0)),
        ((z_lo == 0) & (y == 0), at(3, 0)),
        ((y >= 1) & (z_lo < 3), at(y, z_lo + 1)),
        ((y == 1) & (z_lo >= 1), at(0, z_lo)),
    ]
    back = (y == 0) & (z_lo >= 1)
    parent_y = jnp.where(z_lo == 0, jnp.where(y == 2, 1, 0), jnp.where(y == 0, 1, y))
    parent_z = jnp.where((z_lo == 0) | back, z_lo, z_lo - 1)
    turn = jnp.where(y == 3, 1, y)
    hops = jnp.where(back, z_lo + 2, turn + z_lo)
    return children, at(parent_y, parent_z), hops


def count(children):
    total = 0
    for cond, _ in children:
        total = total + cond.astype(jnp.int32)
    return total


def wait_for(barrier, signals):
    @pl.when(signals > 0)
    def _():
        pl.semaphore_wait(barrier, signals)


def remote(src, dst, send, recv, target):
    return pltpu.make_async_remote_copy(
        src_ref=src, dst_ref=dst, send_sem=send, recv_sem=recv, device_id=target, device_id_type=MESH
    )


def split(value):
    high = value.astype(BF16)
    return high, (value - high.astype(F32)).astype(BF16)


def outer(left, right):
    left_high, left_low = split(left)
    right_high, right_low = split(right)
    dims = ((1,), (1,))
    return dot(left_high, right_high, dims) + (dot(left_high, right_low, dims) + dot(left_low, right_high, dims))


def panel_kernel(a_ref, inv_ref, f_ref, d_ref, l_ref, send, recv, own):
    half, z_hi, x, y, z_lo = place()
    source, children, parent, _ = group_tree(half, z_hi, x, y, z_lo, 0, 0, 0)
    active = (y == 0) & (z_lo == 0)
    barrier = pltpu.get_barrier_semaphore()

    @pl.when(active)
    def _():
        @pl.when(jnp.logical_not(source))
        def _():
            pl.semaphore_signal(barrier, inc=1, device_id=parent, device_id_type=MESH)

        wait_for(barrier, count(children))

        def piece(ref, block):
            return ref.at[pl.ds(block * WIDTH, WIDTH), pl.ds(0, block * WIDTH)]

        def copy(block, number):
            return remote(
                piece(d_ref, block), piece(d_ref, block), send.at[number, block - 1], recv.at[block - 1], children[number][1]
            )

        for block in range(1, BLOCKS):
            @pl.when(source)
            def _():
                mine = pltpu.make_async_copy(piece(a_ref, block), piece(d_ref, block), own)
                mine.start()
                mine.wait()

            @pl.when(jnp.logical_not(source))
            def _():
                copy(block, 0).wait_recv()

            for number, (cond, _) in enumerate(children):
                @pl.when(cond)
                def _():
                    copy(block, number).start()

        lower = lax.broadcasted_iota(jnp.int32, (WIDTH, WIDTH), 0) >= lax.broadcasted_iota(jnp.int32, (WIDTH, WIDTH), 1)
        for block in range(BLOCKS):
            inverse = jnp.where(lower, inv_ref[block], 0.0)
            here = pl.ds(block * WIDTH, WIDTH)
            done = pl.ds(0, block * WIDTH)
            current = a_ref[:, here]
            if block > 0:
                above = l_ref[here, done]
                current = current - outer(f_ref[:, done], above)
            f_ref[:, here] = outer(current, inverse)
            if block + 1 < BLOCKS:
                below = pl.ds((block + 1) * WIDTH, PANEL - (block + 1) * WIDTH)
                current = d_ref[below, here]
                if block > 0:
                    current = current - outer(l_ref[below, done], above)
                l_ref[below, here] = outer(current, inverse)

        for block in range(1, BLOCKS):
            for number, (cond, _) in enumerate(children):
                @pl.when(cond)
                def _():
                    copy(block, number).wait_send()


def panel(a, inverse_blocks):
    return pl.pallas_call(
        panel_kernel,
        out_shape=jax.ShapeDtypeStruct(a.shape, F32),
        in_specs=[pl.BlockSpec(memory_space=pltpu.VMEM)] * 2,
        out_specs=pl.BlockSpec(memory_space=pltpu.VMEM),
        scratch_shapes=[
            pltpu.VMEM((PANEL, PANEL), F32),
            pltpu.VMEM((PANEL, PANEL), F32),
            pltpu.SemaphoreType.DMA((4, BLOCKS - 1)),
            pltpu.SemaphoreType.DMA((BLOCKS - 1,)),
            pltpu.SemaphoreType.DMA,
        ],
        compiler_params=pltpu.CompilerParams(collective_id=0, has_side_effects=True, vmem_limit_bytes=24 * 2**20),
        name="panel",
    )(a, inverse_blocks)


CHUNK = 32
STEP = 2


def spread_kernel(f_ref, row_ref, col_ref, recv_z, recv_y, recv_g, send_z, send_y, send_g, own):
    half, z_hi, x, y, z_lo = place()
    side = row_ref.shape[0] // 2
    chunks = side // CHUNK
    tree_z, parent_z, hops_z = z_first_tree(half, z_hi, x, y, z_lo)
    tree_y, parent_y, hops_y = y_first_tree(half, z_hi, x, y, z_lo)
    root = (y == 0) & (z_lo == 0)
    lead, near = half == y // 2, z_hi == y % 2
    source = lead & near & (x == z_lo)
    column = [
        device(half, 1 - z_hi, x, y, z_lo),
        device(half, z_hi, (x + 1) % 4, y, z_lo),
        device(half, z_hi, (x + 3) % 4, y, z_lo),
        device(1 - half, z_hi, x, y, z_lo),
    ]
    barrier = pltpu.get_barrier_semaphore()

    @pl.when(jnp.logical_not(root))
    def _():
        pl.semaphore_signal(barrier, inc=1, device_id=parent_z, device_id_type=MESH)
        pl.semaphore_signal(barrier, inc=1, device_id=parent_y, device_id_type=MESH)

    for target in column:
        pl.semaphore_signal(barrier, inc=1, device_id=target, device_id_type=MESH)

    @pl.when(root)
    def _():
        mine = pltpu.make_async_copy(f_ref, row_ref, own)
        mine.start()
        mine.wait()

    pl.semaphore_wait(barrier, count(tree_z) + count(tree_y) + len(column))

    def rows(number):
        return pl.ds(pl.multiple_of(number * CHUNK, CHUNK), CHUNK)

    def forward(src, dst, number, tree, sends, recv):
        for slot, (cond, target) in enumerate(tree):
            @pl.when(cond)
            def _():
                remote(src.at[rows(number)], dst.at[rows(number)], sends(slot), recv, target).start()

    def turn(away):
        return jnp.where(away == 3, 1, away)

    def column_tree(bridge):
        from_source = (x - z_lo + 4) % 4
        away = jnp.where(near, from_source, (from_source - bridge + 4) % 4)
        children = [
            (lead & near & (from_source == bridge), column[0]),
            (lead & (away <= 1), column[1]),
            (lead & (away == 0), column[2]),
            (lead, column[3]),
        ]
        hops = turn(away) + jnp.where(lead, 0, 1) + jnp.where(near, 0, 2 + turn(bridge))
        return children, hops

    def along_row(number, offset, tree, sends, recv):
        @pl.when((number >= 0) & (number < chunks))
        def _():
            @pl.when(jnp.logical_not(root))
            def _():
                at = row_ref.at[rows(offset + number)]
                remote(at, at, sends.at[0], recv.at[number], tree[0][1]).wait_recv()

            forward(row_ref, row_ref, offset + number, tree, lambda slot: sends.at[slot], recv.at[number])

            @pl.when(source)
            def _():
                along = offset + number
                forward(row_ref, col_ref, along, column_tree(number % 4)[0], lambda slot: send_g.at[slot, along], recv_g.at[along])

    def along_col(step, offset):
        def one(bridge, carry):
            children, hops = column_tree(bridge)
            number = step - hops * STEP

            @pl.when((number >= 0) & (number < chunks) & (number % 4 == bridge) & jnp.logical_not(source))
            def _():
                along = offset + number
                at = col_ref.at[rows(along)]
                remote(at, at, send_g.at[0, along], recv_g.at[along], column[0]).wait_recv()
                forward(col_ref, col_ref, along, children, lambda slot: send_g.at[slot, along], recv_g.at[along])

            return carry

        lax.fori_loop(0, 4, one, 0)

    start_z, start_y = hops_z * STEP, hops_y * STEP

    def body(step, carry):
        along_row(step - start_z, 0, tree_z, send_z, recv_z)
        along_row(step - start_y, chunks, tree_y, send_y, recv_y)
        along_col(step - start_z, 0)
        along_col(step - start_y, chunks)
        return carry

    lax.fori_loop(0, chunks + STEP * 13, body, 0)

    @pl.when(source)
    def _():
        mine = pltpu.make_async_copy(row_ref, col_ref, own)
        mine.start()
        mine.wait()

    def drain(tree, sends):
        at = row_ref.at[pl.ds(0, side)]
        for slot, (cond, target) in enumerate(tree):
            @pl.when(cond)
            def _():
                remote(at, at, sends.at[slot], recv_z.at[0], target).wait_send()

    drain(tree_z, send_z)
    drain(tree_y, send_y)

    def drain_column(number, carry):
        at = row_ref.at[rows(number)]
        for slot, (cond, target) in enumerate(column_tree(number % 4)[0]):
            @pl.when(cond)
            def _():
                remote(at, at, send_g.at[slot, number], recv_z.at[0], target).wait_send()

        return carry

    lax.fori_loop(0, 2 * chunks, drain_column, 0)


def spread(f):
    chunks = f.shape[0] // 2 // CHUNK
    return pl.pallas_call(
        spread_kernel,
        out_shape=[jax.ShapeDtypeStruct(f.shape, F32)] * 2,
        in_specs=[pl.BlockSpec(memory_space=pltpu.VMEM)],
        out_specs=[pl.BlockSpec(memory_space=pltpu.VMEM)] * 2,
        scratch_shapes=[
            pltpu.SemaphoreType.DMA((chunks,)),
            pltpu.SemaphoreType.DMA((chunks,)),
            pltpu.SemaphoreType.DMA((2 * chunks,)),
            pltpu.SemaphoreType.DMA((4,)),
            pltpu.SemaphoreType.DMA((4,)),
            pltpu.SemaphoreType.DMA((4, 2 * chunks)),
            pltpu.SemaphoreType.DMA,
        ],
        compiler_params=pltpu.CompilerParams(collective_id=1, has_side_effects=True, vmem_limit_bytes=24 * 2**20),
        name="spread",
    )(f)


def exchange_kernel(
    x_ref, parent_ref, row_ref, col_ref, row_land_ref, col_land_ref, out_ref,
    held, strained, passed, packed, landed, pick, by_col, parts, by_row, put,
    own, first, ring_sent, ring_got, less_sent, less_got, sent, got, kept,
):
    half, z_hi, x, y, z_lo = place()
    z = z_hi * 4 + z_lo
    mid = held.shape[1] // 2
    tile = 256
    rows_dims = ((1,), (1,))
    up, down = (z + 1) % 8, (z + 7) % 8
    above = device(half, up // 4, x, y, up % 4)
    below = device(half, down // 4, x, y, down % 4)

    def peer(number):
        return device((half + number // 16) % 2, z_hi, (x + number // 4) % 4, (y + number) % 4, z_lo)

    mine = pltpu.make_async_copy(x_ref, held.at[0], own)
    mine.start()
    front = pltpu.make_async_copy(parent_ref, out_ref, first)
    front.start()
    barrier = pltpu.get_barrier_semaphore()
    for target in (above, below):
        pl.semaphore_signal(barrier, inc=1, device_id=target, device_id_type=MESH)

    def greet(number, carry):
        pl.semaphore_signal(barrier, inc=1, device_id=peer(number), device_id_type=MESH)
        return carry

    lax.fori_loop(1, 32, greet, 0)
    mine.wait()
    pl.semaphore_wait(barrier, 33)

    def at_of(number):
        return jnp.where(number % 2 == 1, 8 - (number + 1) // 2, number // 2)

    def spot(at):
        return at - at // 7 * 3

    def part(at, side):
        return held.at[spot(at), pl.ds(side * mid, mid), :]


    def ring(at, way, side):
        to = (at + 7) % 8 if way == 0 else (at + 1) % 8
        return remote(
            part(at, side), part(to, side), ring_sent.at[way, at, side], ring_got.at[to, side], (above, below)[way]
        )

    def arrived(at, side):
        remote(part(at, side), part(at, side), ring_sent.at[0, at, side], ring_got.at[at, side], above).wait_recv()

    def less(place, way):
        return remote(
            passed.at[place], strained.at[place], less_sent.at[place], less_got.at[place], (above, below)[way]
        )

    def columns_of(which, at, here):
        slots = lax.broadcasted_iota(jnp.int32, (4 * CAP, SUB), 0)
        col_pick = (slots == col_ref[which, (z + at) % 4]).astype(F32).astype(BF16)
        high, low = split(held[spot(at), here, :])
        return dot(col_pick, high, rows_dims), dot(col_pick, low, rows_dims)

    def strain(at, side, way, place):
        high, low = columns_of(1 + way, at, pl.ds(side * mid, mid))
        passed[place] = high + low
        less(place, way).start()

    def message(number, to):
        to_half, to_x, to_y = (half + to // 16) % 2, (x + to // 4) % 4, (y + to) % 4
        src = packed.at[
            number % 4,
            pl.ds(pl.multiple_of(to_y * CAP, CAP), CAP),
            pl.ds(pl.multiple_of((to_half * 4 + to_x) * 128, 128), 128),
        ]
        dst = landed.at[
            at_of(number), half, pl.ds(pl.multiple_of(y * CAP, CAP), CAP), pl.ds(pl.multiple_of(x * 128, 128), 128)
        ]
        return src, dst

    def deliver(number):
        src, dst = message(number, 0)
        pltpu.make_async_copy(src, dst, kept.at[number]).start()

        def one(to, carry):
            src, dst = message(number, to)
            remote(src, dst, sent.at[number], got.at[number], peer(to)).start()
            return carry

        lax.fori_loop(1, 32, one, 0)

    def others():
        return out_ref.at[pl.ds(0, 31 * 8), :]

    def gone(number):
        remote(others(), others(), sent.at[number], got.at[number], above).wait_send()

    def landed_all(number):
        remote(others(), others(), sent.at[number], got.at[number], above).wait_recv()
        src, dst = message(number, 0)
        pltpu.make_async_copy(src, dst, kept.at[number]).wait()

    def pack(number):
        at = at_of(number)
        there = (z + at) % 8
        for side in range(2):
            lanes = pl.ds(side * mid, mid)
            full = (at != 4) & (at != (3, 5)[side])

            @pl.when(full)
            def _():
                high, low = columns_of(0, at, lanes)
                by_col[: 4 * CAP, lanes] = high.astype(BF16)
                by_col[4 * CAP :, lanes] = low.astype(BF16)

            @pl.when(jnp.logical_not(full))
            def _():
                high, low = split(strained[jnp.where(at == 4, 2 + side, 1 - side)])
                by_col[: 4 * CAP, lanes] = high
                by_col[4 * CAP :, lanes] = low

        def rows(step, carry):
            here = pl.ds(pl.multiple_of(step * tile, tile), tile)
            both = dot(by_col[...], pick[there // 4, here, :], rows_dims)
            packed[number % 4, :, here] = both[: 4 * CAP] + both[4 * CAP :]
            return carry

        lax.fori_loop(0, LOC // tile, rows, 0)

    def rows_of(number, child, step):
        source = (z + at_of(number)) % 8 // 4
        places = lax.broadcasted_iota(jnp.int32, (tile, SUB), 0) + step * tile
        row_put = (places == row_land_ref[child, source]).astype(F32).astype(BF16)
        return dot(row_put, parts[child], rows_dims).astype(BF16)

    def take(number):
        landed_all(number)
        for child in range(2):
            high, low = split(landed[at_of(number), child])
            parts[child, : 4 * CAP] = high
            parts[child, 4 * CAP :] = low

    def unpack_first(number):
        take(number)

        def rows(step, carry):
            here = pl.ds(pl.multiple_of(step * tile, tile), tile)
            for child in range(2):
                by_row[at_of(number) % 4, child, here, :] = rows_of(number, child, step)
            return carry

        lax.fori_loop(0, LOC // tile, rows, 0)

    def unpack_second(number, carry):
        source = (z + at_of(number)) % 4
        for child in range(2):
            places = lax.broadcasted_iota(jnp.int32, (LOC, 4 * CAP), 0)
            col_put = (places == col_land_ref[child, source]).astype(F32).astype(BF16)
            put[child, :, : 4 * CAP] = col_put
            put[child, :, 4 * CAP :] = col_put
        take(number)

        def rows(step, carry):
            here = pl.ds(pl.multiple_of(step * tile, tile), tile)
            total = out_ref[here, :]
            for child in range(2):
                both = by_row[at_of(number) % 4, child, here, :] + rows_of(number, child, step)
                total = total + dot(both, put[child], rows_dims)
            out_ref[here, :] = total
            return carry

        lax.fori_loop(0, LOC // tile, rows, 0)
        return carry

    for turn in range(2):
        for way in range(2):
            ring(0, way, (turn + way) % 2).start()
    for source in range(2):
        slots = lax.broadcasted_iota(jnp.int32, pick.shape[1:], 0)
        pick[source] = (slots == row_ref[source]).astype(F32).astype(BF16)
    front.wait()

    def event(number, carry):
        @pl.when(number == 1)
        def _():
            for turn in range(2):
                for way in range(2):
                    at, side = (7, 1)[way], (turn + way) % 2
                    arrived(at, side)
                    ring(at, way, side).start()

        @pl.when(number == 3)
        def _():
            for way in range(2):
                at, side = (6, 2)[way], way
                arrived(at, side)
                ring(at, way, side).start()
            for way in range(2):
                at, side = (6, 2)[way], 1 - way
                arrived(at, side)
                strain(at, side, way, way)

        @pl.when(number == 5)
        def _():
            for way in range(2):
                at, side = (5, 3)[way], way
                arrived(at, side)
                strain(at, side, way, 2 + way)
            for way in range(2):
                less(way, way).wait_recv()

        @pl.when(number == 7)
        def _():
            for way in range(2):
                less(2 + way, way).wait_recv()

        @pl.when(number >= 4)
        def _():
            gone(number - 4)

        pack(number)

        @pl.when((number >= 3) & (number < 7))
        def _():
            unpack_first(number - 3)

        deliver(number)
        return carry

    lax.fori_loop(0, 8, event, 0)
    lax.fori_loop(4, 8, unpack_second, 0)

    def settle(number, carry):
        gone(number)
        return carry

    lax.fori_loop(4, 8, settle, 0)
    for way in range(2):
        for at in ((0, 7), (0, 1))[way]:
            for side in range(2):
                ring(at, way, side).wait_send()
        ring((6, 2)[way], way, way).wait_send()
        less(way, way).wait_send()
        less(2 + way, way).wait_send()


def exchange(block, parent, row_slots, col_slots, row_land, col_land):
    rows, cols = block.shape
    return pl.pallas_call(
        exchange_kernel,
        out_shape=jax.ShapeDtypeStruct(parent.shape, F32),
        in_specs=[pl.BlockSpec(memory_space=pl.ANY)] * 2 + [pl.BlockSpec(memory_space=pltpu.VMEM)] * 4,
        out_specs=pl.BlockSpec(memory_space=pltpu.VMEM),
        scratch_shapes=[
            pltpu.VMEM((7, rows, cols), F32),
            pltpu.VMEM((4, 4 * CAP, SUB), F32),
            pltpu.VMEM((4, 4 * CAP, SUB), F32),
            pltpu.VMEM((4, 4 * CAP, LOC), F32),
            pltpu.VMEM((8, 2, 4 * CAP, SUB), F32),
            pltpu.VMEM((2, LOC, rows), BF16),
            pltpu.VMEM((8 * CAP, LOC), BF16),
            pltpu.VMEM((2, 8 * CAP, SUB), BF16),
            pltpu.VMEM((4, 2, LOC, 8 * CAP), BF16),
            pltpu.VMEM((2, LOC, 8 * CAP), BF16),
            pltpu.SemaphoreType.DMA,
            pltpu.SemaphoreType.DMA,
            pltpu.SemaphoreType.DMA((2, 8, 2)),
            pltpu.SemaphoreType.DMA((8, 2)),
            pltpu.SemaphoreType.DMA((4,)),
            pltpu.SemaphoreType.DMA((4,)),
            pltpu.SemaphoreType.DMA((8,)),
            pltpu.SemaphoreType.DMA((8,)),
            pltpu.SemaphoreType.DMA((8,)),
        ],
        compiler_params=pltpu.CompilerParams(collective_id=2, has_side_effects=True, vmem_limit_bytes=63 * 2**20),
        name="exchange",
    )(block, parent, row_slots, col_slots, row_land, col_land)


def local(parent_front, child_blocks, row_maps, inverse_blocks):
    half, row, col = lax.axis_index("half"), lax.axis_index("row"), lax.axis_index("col")
    group = half * 8 + row
    maps = row_maps.reshape(2, -1, SUB)

    mine = lax.dynamic_index_in_dim(maps, half, 0, keepdims=False)
    shards = mine.reshape(2, 4, 2 * SUB)
    target, rank = send_slots(lax.dynamic_index_in_dim(shards, row % 4, 1, keepdims=False).reshape(4, SUB))
    target, rank = target.reshape(2, 2, SUB), rank.reshape(2, 2, SUB)
    side = jnp.arange(2, dtype=jnp.int32)[:, None]
    slot = (((target // 8) * 4 + target % 4) * 2 + side) * CAP + rank
    row_slots = jnp.where(target // 4 % 2 == row // 4, slot, -1).reshape(2, 1, 2 * SUB)
    target, rank = send_slots(lax.dynamic_index_in_dim(mine.reshape(4, 4, SUB), col // 4, 0, keepdims=False))
    stops = (col + jnp.array([0, 1, 3], jnp.int32))[:, None, None] % 4
    col_slots = jnp.where(target % 4 == stops, (target // 4) * CAP + rank, -1).reshape(3, 4, 1, SUB)

    row_land = landing(maps, group).reshape(2, 2, 1, SUB)
    col_land = landing(maps, col).reshape(2, 4, 4, CAP).transpose(0, 2, 1, 3).reshape(2, 4, 1, 4 * CAP)
    assembled = exchange(child_blocks[0], parent_front, row_slots, col_slots, row_land, col_land)

    factor = panel(assembled[:, :PANEL], inverse_blocks)
    factor_rows, factor_cols = spread(factor)
    product = lax.dot_general(
        factor_rows, factor_cols, (((1,), (1,)), ((), ())), precision=lax.Precision.HIGH, preferred_element_type=F32
    )
    return assembled - product, factor_rows.astype(BF16)


def solution(mesh):
    in_specs = (P(("half", "row"), "col"), P("half", "row", "col"), P(), P())
    out_specs = (P(("half", "row"), "col"), P(("half", "row"), None))
    return jax.shard_map(local, mesh=mesh, in_specs=in_specs, out_specs=out_specs, check_vma=False)
```

```python
import functools

import jax
import jax.numpy as jnp
from jax import lax
from jax.experimental import pallas as pl
from jax.experimental.pallas import tpu as pltpu
from jax.sharding import PartitionSpec as P

MESH = pl.DeviceIdType.MESH
F32 = jnp.float32
BF16 = jnp.bfloat16

SUB = 512
CAP = 64
LOC = 1024
GROUPS = 16
WIDTH = 128
BLOCKS = 4
PANEL = WIDTH * BLOCKS


def dot(left, right, dims):
    return lax.dot_general(left, right, (dims, ((), ())), preferred_element_type=F32)


def place():
    half, row, col = lax.axis_index("half"), lax.axis_index("row"), lax.axis_index("col")
    return half, row // 4, row % 4, col // 4, col % 4


def device(half, z_hi, x, y, z_lo):
    return {"half": half, "row": z_hi * 4 + x, "col": y * 4 + z_lo}


def group_tree(half, z_hi, x, y, z_lo, src_half, src_z, src_x):
    away = (x - src_x + 4) % 4
    lead = half == src_half
    source = lead & (z_hi == src_z) & (away == 0)
    children = [
        (source, device(half, 1 - z_hi, x, y, z_lo)),
        (lead & (away <= 1), device(half, z_hi, (x + 1) % 4, y, z_lo)),
        (lead & (away == 0), device(half, z_hi, (x + 3) % 4, y, z_lo)),
        (lead, device(1 - half, z_hi, x, y, z_lo)),
    ]
    up_x = jnp.where(away == 3, (x + 1) % 4, (x + 3) % 4)
    parent_half = jnp.where(lead, half, 1 - half)
    parent_z = jnp.where(lead & (away == 0), 1 - z_hi, z_hi)
    parent_x = jnp.where(lead & (away != 0), up_x, x)
    parent = device(parent_half, parent_z, parent_x, y, z_lo)
    hops = jnp.where(away == 3, 1, away) + jnp.where(lead, 0, 1) + jnp.where(z_hi == src_z, 0, 2)
    return source, children, parent, hops


def z_first_tree(half, z_hi, x, y, z_lo):
    at = lambda y2, z2: device(half, z_hi, x, y2, z2)
    children = [
        ((y == 0) & (z_lo < 3), at(0, z_lo + 1)),
        ((y <= 1) & (z_lo >= 1), at(y + 1, z_lo)),
        ((y == 0) & (z_lo >= 1), at(3, z_lo)),
        ((y >= 1) & (z_lo == 1), at(y, 0)),
    ]
    back = (z_lo == 0) & (y >= 1)
    parent_y = jnp.where(back, y, jnp.where(y == 2, 1, 0))
    parent_z = jnp.where(back, 1, jnp.where(y == 0, z_lo - 1, z_lo))
    turn = jnp.where(y == 3, 1, y)
    hops = jnp.where(back, turn + 2, turn + z_lo)
    return children, at(parent_y, parent_z), hops


def y_first_tree(half, z_hi, x, y, z_lo):
    at = lambda y2, z2: device(half, z_hi, x, y2, z2)
    children = [
        ((z_lo == 0) & (y <= 1), at(y + 1, 0)),
        ((z_lo == 0) & (y == 0), at(3, 0)),
        ((y >= 1) & (z_lo < 3), at(y, z_lo + 1)),
        ((y == 1) & (z_lo >= 1), at(0, z_lo)),
    ]
    back = (y == 0) & (z_lo >= 1)
    parent_y = jnp.where(z_lo == 0, jnp.where(y == 2, 1, 0), jnp.where(y == 0, 1, y))
    parent_z = jnp.where((z_lo == 0) | back, z_lo, z_lo - 1)
    turn = jnp.where(y == 3, 1, y)
    hops = jnp.where(back, z_lo + 2, turn + z_lo)
    return children, at(parent_y, parent_z), hops


def count(children):
    total = 0
    for cond, _ in children:
        total = total + cond.astype(jnp.int32)
    return total


def wait_for(barrier, signals):
    @pl.when(signals > 0)
    def _():
        pl.semaphore_wait(barrier, signals)


def remote(src, dst, send, recv, target):
    return pltpu.make_async_remote_copy(
        src_ref=src, dst_ref=dst, send_sem=send, recv_sem=recv, device_id=target, device_id_type=MESH
    )


def split(value):
    high = value.astype(BF16)
    return high, (value - high.astype(F32)).astype(BF16)


def outer(left, right):
    left_high, left_low = split(left)
    right_high, right_low = split(right)
    dims = ((1,), (1,))
    return dot(left_high, right_high, dims) + (dot(left_high, right_low, dims) + dot(left_low, right_high, dims))


def panel_kernel(front_ref, inv_ref, f_ref, a_ref, d_ref, l_ref, send, recv, own, first):
    half, z_hi, x, y, z_lo = place()
    source, children, parent, _ = group_tree(half, z_hi, x, y, z_lo, 0, 0, 0)
    active = (y == 0) & (z_lo == 0)
    barrier = pltpu.get_barrier_semaphore()

    @pl.when(active)
    def _():
        mine = pltpu.make_async_copy(front_ref.at[:, pl.ds(0, PANEL)], a_ref, first)
        mine.start()

        @pl.when(jnp.logical_not(source))
        def _():
            pl.semaphore_signal(barrier, inc=1, device_id=parent, device_id_type=MESH)

        mine.wait()
        wait_for(barrier, count(children))

        def piece(ref, block):
            return ref.at[pl.ds(block * WIDTH, WIDTH), pl.ds(0, block * WIDTH)]

        def copy(block, number):
            return remote(
                piece(d_ref, block), piece(d_ref, block), send.at[number, block - 1], recv.at[block - 1], children[number][1]
            )

        for block in range(1, BLOCKS):
            @pl.when(source)
            def _():
                copied = pltpu.make_async_copy(piece(a_ref, block), piece(d_ref, block), own)
                copied.start()
                copied.wait()

            @pl.when(jnp.logical_not(source))
            def _():
                copy(block, 0).wait_recv()

            for number, (cond, _) in enumerate(children):
                @pl.when(cond)
                def _():
                    copy(block, number).start()

        lower = lax.broadcasted_iota(jnp.int32, (WIDTH, WIDTH), 0) >= lax.broadcasted_iota(jnp.int32, (WIDTH, WIDTH), 1)
        for block in range(BLOCKS):
            inverse = jnp.where(lower, inv_ref[block], 0.0)
            here = pl.ds(block * WIDTH, WIDTH)
            done = pl.ds(0, block * WIDTH)
            current = a_ref[:, here]
            if block > 0:
                above = l_ref[here, done]
                current = current - outer(f_ref[:, done], above)
            f_ref[:, here] = outer(current, inverse)
            if block + 1 < BLOCKS:
                below = pl.ds((block + 1) * WIDTH, PANEL - (block + 1) * WIDTH)
                current = d_ref[below, here]
                if block > 0:
                    current = current - outer(l_ref[below, done], above)
                l_ref[below, here] = outer(current, inverse)

        for block in range(1, BLOCKS):
            for number, (cond, _) in enumerate(children):
                @pl.when(cond)
                def _():
                    copy(block, number).wait_send()


def panel(front, inverse_blocks):
    return pl.pallas_call(
        panel_kernel,
        out_shape=jax.ShapeDtypeStruct((LOC, PANEL), F32),
        in_specs=[pl.BlockSpec(memory_space=pl.ANY), pl.BlockSpec(memory_space=pltpu.VMEM)],
        out_specs=pl.BlockSpec(memory_space=pltpu.VMEM),
        scratch_shapes=[
            pltpu.VMEM((LOC, PANEL), F32),
            pltpu.VMEM((PANEL, PANEL), F32),
            pltpu.VMEM((PANEL, PANEL), F32),
            pltpu.SemaphoreType.DMA((4, BLOCKS - 1)),
            pltpu.SemaphoreType.DMA((BLOCKS - 1,)),
            pltpu.SemaphoreType.DMA,
            pltpu.SemaphoreType.DMA,
        ],
        compiler_params=pltpu.CompilerParams(collective_id=0, has_side_effects=True, vmem_limit_bytes=24 * 2**20),
        name="panel",
    )(front, inverse_blocks)


CHUNK = 16
STEP = 3


def spread_kernel(f_ref, row_ref, col_ref, recv_z, recv_y, recv_g, send_z, send_y, send_g, own):
    half, z_hi, x, y, z_lo = place()
    side = row_ref.shape[0] // 2
    chunks = side // CHUNK
    tree_z, parent_z, hops_z = z_first_tree(half, z_hi, x, y, z_lo)
    tree_y, parent_y, hops_y = y_first_tree(half, z_hi, x, y, z_lo)
    root = (y == 0) & (z_lo == 0)
    lead, near = half == y // 2, z_hi == y % 2
    source = lead & near & (x == z_lo)
    column = [
        device(half, 1 - z_hi, x, y, z_lo),
        device(half, z_hi, (x + 1) % 4, y, z_lo),
        device(half, z_hi, (x + 3) % 4, y, z_lo),
        device(1 - half, z_hi, x, y, z_lo),
    ]
    barrier = pltpu.get_barrier_semaphore()

    @pl.when(jnp.logical_not(root))
    def _():
        pl.semaphore_signal(barrier, inc=1, device_id=parent_z, device_id_type=MESH)
        pl.semaphore_signal(barrier, inc=1, device_id=parent_y, device_id_type=MESH)

    for target in column:
        pl.semaphore_signal(barrier, inc=1, device_id=target, device_id_type=MESH)

    @pl.when(root)
    def _():
        mine = pltpu.make_async_copy(f_ref, row_ref, own)
        mine.start()
        mine.wait()

    pl.semaphore_wait(barrier, count(tree_z) + count(tree_y) + len(column))

    def rows(number):
        return pl.ds(pl.multiple_of(number * CHUNK, CHUNK), CHUNK)

    def forward(src, dst, number, tree, sends, recv):
        for slot, (cond, target) in enumerate(tree):
            @pl.when(cond)
            def _():
                remote(src.at[rows(number)], dst.at[rows(number)], sends(slot), recv, target).start()

    def turn(away):
        return jnp.where(away == 3, 1, away)

    def column_tree(bridge):
        from_source = (x - z_lo + 4) % 4
        away = jnp.where(near, from_source, (from_source - bridge + 4) % 4)
        children = [
            (lead & near & (from_source == bridge), column[0]),
            (lead & (away <= 1), column[1]),
            (lead & (away == 0), column[2]),
            (lead, column[3]),
        ]
        hops = turn(away) + jnp.where(lead, 0, 1) + jnp.where(near, 0, 2 + turn(bridge))
        return children, hops

    def along_row(number, offset, tree, sends, recv):
        @pl.when((number >= 0) & (number < chunks))
        def _():
            @pl.when(jnp.logical_not(root))
            def _():
                at = row_ref.at[rows(offset + number)]
                remote(at, at, sends.at[0], recv.at[number], tree[0][1]).wait_recv()

            forward(row_ref, row_ref, offset + number, tree, lambda slot: sends.at[slot], recv.at[number])

            @pl.when(source)
            def _():
                along = offset + number
                forward(row_ref, col_ref, along, column_tree(number % 4)[0], lambda slot: send_g.at[slot, along], recv_g.at[along])

    def along_col(step, offset):
        def one(bridge, carry):
            children, hops = column_tree(bridge)
            number = step - hops * STEP

            @pl.when((number >= 0) & (number < chunks) & (number % 4 == bridge) & jnp.logical_not(source))
            def _():
                along = offset + number
                at = col_ref.at[rows(along)]
                remote(at, at, send_g.at[0, along], recv_g.at[along], column[0]).wait_recv()
                forward(col_ref, col_ref, along, children, lambda slot: send_g.at[slot, along], recv_g.at[along])

            return carry

        lax.fori_loop(0, 4, one, 0)

    start_z, start_y = hops_z * STEP, hops_y * STEP

    def body(step, carry):
        along_row(step - start_z, 0, tree_z, send_z, recv_z)
        along_row(step - start_y, chunks, tree_y, send_y, recv_y)
        along_col(step - start_z, 0)
        along_col(step - start_y, chunks)
        return carry

    lax.fori_loop(0, chunks + STEP * 13, body, 0)

    @pl.when(source)
    def _():
        mine = pltpu.make_async_copy(row_ref, col_ref, own)
        mine.start()
        mine.wait()

    def drain(tree, sends):
        at = row_ref.at[pl.ds(0, side)]
        for slot, (cond, target) in enumerate(tree):
            @pl.when(cond)
            def _():
                remote(at, at, sends.at[slot], recv_z.at[0], target).wait_send()

    drain(tree_z, send_z)
    drain(tree_y, send_y)

    def drain_column(number, carry):
        at = row_ref.at[rows(number)]
        for slot, (cond, target) in enumerate(column_tree(number % 4)[0]):
            @pl.when(cond)
            def _():
                remote(at, at, send_g.at[slot, number], recv_z.at[0], target).wait_send()

        return carry

    lax.fori_loop(0, 2 * chunks, drain_column, 0)


def spread(f):
    chunks = f.shape[0] // 2 // CHUNK
    return pl.pallas_call(
        spread_kernel,
        out_shape=[jax.ShapeDtypeStruct(f.shape, F32)] * 2,
        in_specs=[pl.BlockSpec(memory_space=pltpu.VMEM)],
        out_specs=[pl.BlockSpec(memory_space=pltpu.VMEM)] * 2,
        scratch_shapes=[
            pltpu.SemaphoreType.DMA((chunks,)),
            pltpu.SemaphoreType.DMA((chunks,)),
            pltpu.SemaphoreType.DMA((2 * chunks,)),
            pltpu.SemaphoreType.DMA((4,)),
            pltpu.SemaphoreType.DMA((4,)),
            pltpu.SemaphoreType.DMA((4, 2 * chunks)),
            pltpu.SemaphoreType.DMA,
        ],
        compiler_params=pltpu.CompilerParams(collective_id=1, has_side_effects=True, vmem_limit_bytes=24 * 2**20),
        name="spread",
    )(f)


def exchange_kernel(
    x_ref, parent_ref, maps_ref, out_ref,
    col_ref, row_land_ref, col_land_ref, upper, held, strained, passed, packed, landed, pick, by_col, parts, by_row, put,
    own, first, ring_sent, ring_got, less_sent, less_got, sent, got, kept,
):
    half, z_hi, x, y, z_lo = place()
    z = z_hi * 4 + z_lo
    mid = held.shape[1] // 2
    tile = 256
    rows_dims = ((1,), (1,))
    up, down = (z + 1) % 8, (z + 7) % 8
    above = device(half, up // 4, x, y, up % 4)
    below = device(half, down // 4, x, y, down % 4)

    def peer(number):
        return device((half + number // 16) % 2, z_hi, (x + number // 4) % 4, (y + number) % 4, z_lo)

    mine = pltpu.make_async_copy(x_ref, held.at[0], own)
    mine.start()
    front = pltpu.make_async_copy(parent_ref, out_ref, first)
    front.start()
    barrier = pltpu.get_barrier_semaphore()
    for target in (above, below):
        pl.semaphore_signal(barrier, inc=1, device_id=target, device_id_type=MESH)

    def greet(number, carry):
        pl.semaphore_signal(barrier, inc=1, device_id=peer(number), device_id_type=MESH)
        return carry

    lax.fori_loop(1, 32, greet, 0)
    mine.wait()
    pl.semaphore_wait(barrier, 33)

    def at_of(number):
        return jnp.where(number % 2 == 1, 8 - (number + 1) // 2, number // 2)

    def spot(at):
        return at - at // 7 * 3

    def part(at, side):
        return held.at[spot(at), pl.ds(side * mid, mid), :]


    def ring(at, way, side):
        to = (at + 7) % 8 if way == 0 else (at + 1) % 8
        return remote(
            part(at, side), part(to, side), ring_sent.at[way, at, side], ring_got.at[to, side], (above, below)[way]
        )

    def arrived(at, side):
        remote(part(at, side), part(at, side), ring_sent.at[0, at, side], ring_got.at[at, side], above).wait_recv()

    def less(place, way):
        return remote(
            passed.at[place], strained.at[place], less_sent.at[place], less_got.at[place], (above, below)[way]
        )

    def columns_of(which, at, here):
        slots = lax.broadcasted_iota(jnp.int32, (4 * CAP, SUB), 0)
        col_pick = (slots == col_ref[which, (z + at) % 4]).astype(F32).astype(BF16)
        high, low = split(held[spot(at), here, :])
        return dot(col_pick, high, rows_dims), dot(col_pick, low, rows_dims)

    def strain(at, side, way, place):
        high, low = columns_of(1 + way, at, pl.ds(side * mid, mid))
        passed[place] = high + low
        less(place, way).start()

    def message(number, to):
        to_half, to_x, to_y = (half + to // 16) % 2, (x + to // 4) % 4, (y + to) % 4
        src = packed.at[
            number % 4,
            pl.ds(pl.multiple_of(to_y * CAP, CAP), CAP),
            pl.ds(pl.multiple_of((to_half * 4 + to_x) * 128, 128), 128),
        ]
        dst = landed.at[
            at_of(number), half, pl.ds(pl.multiple_of(y * CAP, CAP), CAP), pl.ds(pl.multiple_of(x * 128, 128), 128)
        ]
        return src, dst

    def deliver(number):
        src, dst = message(number, 0)
        pltpu.make_async_copy(src, dst, kept.at[number]).start()

        def one(to, carry):
            src, dst = message(number, to)
            remote(src, dst, sent.at[number], got.at[number], peer(to)).start()
            return carry

        lax.fori_loop(1, 32, one, 0)

    def others():
        return out_ref.at[pl.ds(0, 31 * 8), :]

    def gone(number):
        remote(others(), others(), sent.at[number], got.at[number], above).wait_send()

    def landed_all(number):
        remote(others(), others(), sent.at[number], got.at[number], above).wait_recv()
        src, dst = message(number, 0)
        pltpu.make_async_copy(src, dst, kept.at[number]).wait()

    def pack(number):
        at = at_of(number)
        there = (z + at) % 8
        for side in range(2):
            lanes = pl.ds(side * mid, mid)
            full = (at != 4) & (at != (3, 5)[side])

            @pl.when(full)
            def _():
                high, low = columns_of(0, at, lanes)
                by_col[: 4 * CAP, lanes] = high.astype(BF16)
                by_col[4 * CAP :, lanes] = low.astype(BF16)

            @pl.when(jnp.logical_not(full))
            def _():
                high, low = split(strained[jnp.where(at == 4, 2 + side, 1 - side)])
                by_col[: 4 * CAP, lanes] = high
                by_col[4 * CAP :, lanes] = low

        def rows(step, carry):
            here = pl.ds(pl.multiple_of(step * tile, tile), tile)
            both = dot(by_col[...], pick[there // 4, here, :], rows_dims)
            packed[number % 4, :, here] = both[: 4 * CAP] + both[4 * CAP :]
            return carry

        lax.fori_loop(0, LOC // tile, rows, 0)

    def rows_of(number, child, step):
        source = (z + at_of(number)) % 8 // 4
        places = lax.broadcasted_iota(jnp.int32, (tile, SUB), 0) + step * tile
        row_put = (places == row_land_ref[child, source]).astype(F32).astype(BF16)
        return dot(row_put, parts[child], rows_dims).astype(BF16)

    def take(number):
        landed_all(number)
        for child in range(2):
            high, low = split(landed[at_of(number), child])
            parts[child, : 4 * CAP] = high
            parts[child, 4 * CAP :] = low

    def unpack_first(number):
        take(number)

        def rows(step, carry):
            here = pl.ds(pl.multiple_of(step * tile, tile), tile)
            for child in range(2):
                by_row[at_of(number) % 4, child, here, :] = rows_of(number, child, step)
            return carry

        lax.fori_loop(0, LOC // tile, rows, 0)

    def unpack_second(number, carry):
        source = (z + at_of(number)) % 4
        for child in range(2):
            places = lax.broadcasted_iota(jnp.int32, (LOC, 4 * CAP), 0)
            col_put = (places == col_land_ref[child, source]).astype(F32).astype(BF16)
            put[child, :, : 4 * CAP] = col_put
            put[child, :, 4 * CAP :] = col_put
        take(number)

        def rows(step, carry):
            here = pl.ds(pl.multiple_of(step * tile, tile), tile)
            total = out_ref[here, :]
            for child in range(2):
                both = by_row[at_of(number) % 4, child, here, :] + rows_of(number, child, step)
                total = total + dot(both, put[child], rows_dims)
            out_ref[here, :] = total
            return carry

        lax.fori_loop(0, LOC // tile, rows, 0)
        return carry

    for turn in range(2):
        for way in range(2):
            ring(0, way, (turn + way) % 2).start()
    upper[...] = (
        lax.broadcasted_iota(jnp.int32, (SUB, SUB), 0) < lax.broadcasted_iota(jnp.int32, (SUB, SUB), 1)
    ).astype(F32).astype(BF16)

    def before(member):
        return dot(member.astype(F32).astype(BF16), upper[...], ((1,), (0,)))

    def send_slots(parents):
        targets = parents >> 10
        member = targets == lax.broadcasted_iota(jnp.int32, (GROUPS, SUB), 0)
        rank = jnp.sum(jnp.where(member, before(member), 0.0), axis=0, keepdims=True)
        return targets, rank.astype(jnp.int32)

    for source in range(2):
        for sub in range(2):
            targets, rank = send_slots(maps_ref[half, pl.ds(source * 8 + x * 2 + sub, 1), :])
            slot = (((targets >> 3) * 4 + (targets & 3)) * 2 + sub) * CAP + rank
            slot = jnp.where(((targets >> 2) & 1) == z_hi, slot, -1)
            slots = lax.broadcasted_iota(jnp.int32, (LOC, SUB), 0)
            pick[source, :, sub * SUB : (sub + 1) * SUB] = (slots == slot).astype(F32).astype(BF16)
    for source in range(4):
        targets, rank = send_slots(maps_ref[half, pl.ds(y * 4 + source, 1), :])
        for which, stop in enumerate((0, 1, 3)):
            slot = (targets >> 2) * CAP + rank
            col_ref[which, source] = jnp.where((targets & 3) == (z_lo + stop) % 4, slot, -1)

    def landing(child, mine, store):
        parents = maps_ref[child]
        member = (parents >> 10) == mine
        rank = jnp.where(member, before(member).astype(jnp.int32), -1)
        place = (parents & (LOC - 1)) + 1
        slots = lax.broadcasted_iota(jnp.int32, (2 * CAP, SUB), 0)
        line = lax.broadcasted_iota(jnp.int32, (8, SUB), 0)

        def side(block, shift):
            values = place[block : block + 1]
            values = jnp.where(line == 0, values >> 5, jnp.where(line == 1, values & 31, 0)).astype(F32).astype(BF16)
            mine_rank = rank[block : block + 1]
            hit = slots == jnp.where(mine_rank < 0, -1, mine_rank + shift)
            return dot(values, hit.astype(F32).astype(BF16), rows_dims)

        store(lambda first, second: (lambda both: (both[0:1] * 32.0 + both[1:2]).astype(jnp.int32) - 1)(
            side(first, 0) + side(second, CAP)
        ))

    for child in range(2):
        def rows_land(pair):
            for source in range(2):
                for at_x in range(4):
                    block = source * 8 + at_x * 2
                    row_land_ref[child, source, :, at_x * 128 : (at_x + 1) * 128] = pair(block, block + 1)

        def cols_land(pair):
            for source in range(4):
                for at_y in range(2):
                    col_land_ref[child, source, :, at_y * 128 : (at_y + 1) * 128] = pair(
                        at_y * 8 + source, at_y * 8 + 4 + source
                    )

        landing(child, half * 8 + z_hi * 4 + x, rows_land)
        landing(child, y * 4 + z_lo, cols_land)
    front.wait()

    def event(number, carry):
        @pl.when(number == 1)
        def _():
            for turn in range(2):
                for way in range(2):
                    at, side = (7, 1)[way], (turn + way) % 2
                    arrived(at, side)
                    ring(at, way, side).start()

        @pl.when(number == 3)
        def _():
            for way in range(2):
                at, side = (6, 2)[way], way
                arrived(at, side)
                ring(at, way, side).start()
            for way in range(2):
                at, side = (6, 2)[way], 1 - way
                arrived(at, side)
                strain(at, side, way, way)

        @pl.when(number == 5)
        def _():
            for way in range(2):
                at, side = (5, 3)[way], way
                arrived(at, side)
                strain(at, side, way, 2 + way)
            for way in range(2):
                less(way, way).wait_recv()

        @pl.when(number == 7)
        def _():
            for way in range(2):
                less(2 + way, way).wait_recv()

        @pl.when(number >= 4)
        def _():
            gone(number - 4)

        pack(number)

        @pl.when((number >= 3) & (number < 7))
        def _():
            unpack_first(number - 3)

        deliver(number)
        return carry

    lax.fori_loop(0, 8, event, 0)
    lax.fori_loop(4, 8, unpack_second, 0)

    def settle(number, carry):
        gone(number)
        return carry

    lax.fori_loop(4, 8, settle, 0)
    for way in range(2):
        for at in ((0, 7), (0, 1))[way]:
            for side in range(2):
                ring(at, way, side).wait_send()
        ring((6, 2)[way], way, way).wait_send()
        less(way, way).wait_send()
        less(2 + way, way).wait_send()


def exchange(block, parent, maps):
    rows, cols = block.shape
    return pl.pallas_call(
        exchange_kernel,
        out_shape=jax.ShapeDtypeStruct(parent.shape, F32),
        in_specs=[pl.BlockSpec(memory_space=pl.ANY)] * 2 + [pl.BlockSpec(memory_space=pltpu.VMEM)],
        out_specs=pl.BlockSpec(memory_space=pltpu.VMEM),
        scratch_shapes=[
            pltpu.VMEM((3, 4, 1, SUB), jnp.int32),
            pltpu.VMEM((2, 2, 1, SUB), jnp.int32),
            pltpu.VMEM((2, 4, 1, 4 * CAP), jnp.int32),
            pltpu.VMEM((SUB, SUB), BF16),
            pltpu.VMEM((7, rows, cols), F32),
            pltpu.VMEM((4, 4 * CAP, SUB), F32),
            pltpu.VMEM((4, 4 * CAP, SUB), F32),
            pltpu.VMEM((4, 4 * CAP, LOC), F32),
            pltpu.VMEM((8, 2, 4 * CAP, SUB), F32),
            pltpu.VMEM((2, LOC, rows), BF16),
            pltpu.VMEM((8 * CAP, LOC), BF16),
            pltpu.VMEM((2, 8 * CAP, SUB), BF16),
            pltpu.VMEM((4, 2, LOC, 8 * CAP), BF16),
            pltpu.VMEM((2, LOC, 8 * CAP), BF16),
            pltpu.SemaphoreType.DMA,
            pltpu.SemaphoreType.DMA,
            pltpu.SemaphoreType.DMA((2, 8, 2)),
            pltpu.SemaphoreType.DMA((8, 2)),
            pltpu.SemaphoreType.DMA((4,)),
            pltpu.SemaphoreType.DMA((4,)),
            pltpu.SemaphoreType.DMA((8,)),
            pltpu.SemaphoreType.DMA((8,)),
            pltpu.SemaphoreType.DMA((8,)),
        ],
        compiler_params=pltpu.CompilerParams(collective_id=2, has_side_effects=True, vmem_limit_bytes=63 * 2**20),
        name="exchange",
    )(block, parent, maps)


def local(parent_front, child_blocks, row_maps, inverse_blocks):
    assembled = exchange(child_blocks[0], parent_front, row_maps.reshape(2, -1, SUB))
    factor = panel(assembled, inverse_blocks)
    factor_rows, factor_cols = spread(factor)
    product = lax.dot_general(
        factor_rows, factor_cols, (((1,), (1,)), ((), ())), precision=lax.Precision.HIGH, preferred_element_type=F32
    )
    return assembled - product, factor_rows.astype(BF16)


def solution(mesh):
    in_specs = (P(("half", "row"), "col"), P("half", "row", "col"), P(), P())
    out_specs = (P(("half", "row"), "col"), P(("half", "row"), None))
    return jax.shard_map(local, mesh=mesh, in_specs=in_specs, out_specs=out_specs, check_vma=False)
```

```python
import functools

import jax
import jax.numpy as jnp
from jax import lax
from jax.experimental import pallas as pl
from jax.experimental.pallas import tpu as pltpu
from jax.sharding import PartitionSpec as P

MESH = pl.DeviceIdType.MESH
F32 = jnp.float32
BF16 = jnp.bfloat16

SUB = 512
CAP = 64
LOC = 1024
GROUPS = 16
WIDTH = 128
BLOCKS = 4
PANEL = WIDTH * BLOCKS


def dot(left, right, dims):
    return lax.dot_general(left, right, (dims, ((), ())), preferred_element_type=F32)


def place():
    half, row, col = lax.axis_index("half"), lax.axis_index("row"), lax.axis_index("col")
    return half, row // 4, row % 4, col // 4, col % 4


def device(half, z_hi, x, y, z_lo):
    return {"half": half, "row": z_hi * 4 + x, "col": y * 4 + z_lo}


def group_tree(half, z_hi, x, y, z_lo, src_half, src_z, src_x):
    away = (x - src_x + 4) % 4
    lead = half == src_half
    source = lead & (z_hi == src_z) & (away == 0)
    children = [
        (source, device(half, 1 - z_hi, x, y, z_lo)),
        (lead & (away <= 1), device(half, z_hi, (x + 1) % 4, y, z_lo)),
        (lead & (away == 0), device(half, z_hi, (x + 3) % 4, y, z_lo)),
        (lead, device(1 - half, z_hi, x, y, z_lo)),
    ]
    up_x = jnp.where(away == 3, (x + 1) % 4, (x + 3) % 4)
    parent_half = jnp.where(lead, half, 1 - half)
    parent_z = jnp.where(lead & (away == 0), 1 - z_hi, z_hi)
    parent_x = jnp.where(lead & (away != 0), up_x, x)
    parent = device(parent_half, parent_z, parent_x, y, z_lo)
    hops = jnp.where(away == 3, 1, away) + jnp.where(lead, 0, 1) + jnp.where(z_hi == src_z, 0, 2)
    return source, children, parent, hops


def z_first_tree(half, z_hi, x, y, z_lo):
    at = lambda y2, z2: device(half, z_hi, x, y2, z2)
    children = [
        ((y == 0) & (z_lo < 3), at(0, z_lo + 1)),
        ((y <= 1) & (z_lo >= 1), at(y + 1, z_lo)),
        ((y == 0) & (z_lo >= 1), at(3, z_lo)),
        ((y >= 1) & (z_lo == 1), at(y, 0)),
    ]
    back = (z_lo == 0) & (y >= 1)
    parent_y = jnp.where(back, y, jnp.where(y == 2, 1, 0))
    parent_z = jnp.where(back, 1, jnp.where(y == 0, z_lo - 1, z_lo))
    turn = jnp.where(y == 3, 1, y)
    hops = jnp.where(back, turn + 2, turn + z_lo)
    return children, at(parent_y, parent_z), hops


def y_first_tree(half, z_hi, x, y, z_lo):
    at = lambda y2, z2: device(half, z_hi, x, y2, z2)
    children = [
        ((z_lo == 0) & (y <= 1), at(y + 1, 0)),
        ((z_lo == 0) & (y == 0), at(3, 0)),
        ((y >= 1) & (z_lo < 3), at(y, z_lo + 1)),
        ((y == 1) & (z_lo >= 1), at(0, z_lo)),
    ]
    back = (y == 0) & (z_lo >= 1)
    parent_y = jnp.where(z_lo == 0, jnp.where(y == 2, 1, 0), jnp.where(y == 0, 1, y))
    parent_z = jnp.where((z_lo == 0) | back, z_lo, z_lo - 1)
    turn = jnp.where(y == 3, 1, y)
    hops = jnp.where(back, z_lo + 2, turn + z_lo)
    return children, at(parent_y, parent_z), hops


def count(children):
    total = 0
    for cond, _ in children:
        total = total + cond.astype(jnp.int32)
    return total


def wait_for(barrier, signals):
    @pl.when(signals > 0)
    def _():
        pl.semaphore_wait(barrier, signals)


def remote(src, dst, send, recv, target):
    return pltpu.make_async_remote_copy(
        src_ref=src, dst_ref=dst, send_sem=send, recv_sem=recv, device_id=target, device_id_type=MESH
    )


def split(value):
    high = value.astype(BF16)
    return high, (value - high.astype(F32)).astype(BF16)


def outer(left, right):
    left_high, left_low = split(left)
    right_high, right_low = split(right)
    dims = ((1,), (1,))
    return dot(left_high, right_high, dims) + (dot(left_high, right_low, dims) + dot(left_low, right_high, dims))


def panel_kernel(a_ref, inv_ref, f_ref, d_ref, l_ref, send, recv, own):
    half, z_hi, x, y, z_lo = place()
    source, children, parent, _ = group_tree(half, z_hi, x, y, z_lo, 0, 0, 0)
    active = (y == 0) & (z_lo == 0)
    barrier = pltpu.get_barrier_semaphore()

    @pl.when(active)
    def _():
        @pl.when(jnp.logical_not(source))
        def _():
            pl.semaphore_signal(barrier, inc=1, device_id=parent, device_id_type=MESH)

        wait_for(barrier, count(children))

        def piece(ref, block):
            return ref.at[pl.ds(block * WIDTH, WIDTH), pl.ds(0, block * WIDTH)]

        def copy(block, number):
            return remote(
                piece(d_ref, block), piece(d_ref, block), send.at[number, block - 1], recv.at[block - 1], children[number][1]
            )

        for block in range(1, BLOCKS):
            @pl.when(source)
            def _():
                copied = pltpu.make_async_copy(piece(a_ref, block), piece(d_ref, block), own)
                copied.start()
                copied.wait()

            @pl.when(jnp.logical_not(source))
            def _():
                copy(block, 0).wait_recv()

            for number, (cond, _) in enumerate(children):
                @pl.when(cond)
                def _():
                    copy(block, number).start()

        lower = lax.broadcasted_iota(jnp.int32, (WIDTH, WIDTH), 0) >= lax.broadcasted_iota(jnp.int32, (WIDTH, WIDTH), 1)
        for block in range(BLOCKS):
            inverse = jnp.where(lower, inv_ref[block], 0.0)
            here = pl.ds(block * WIDTH, WIDTH)
            done = pl.ds(0, block * WIDTH)
            current = a_ref[:, here]
            if block > 0:
                above = l_ref[here, done]
                current = current - outer(f_ref[:, done], above)
            f_ref[:, here] = outer(current, inverse)
            if block + 1 < BLOCKS:
                below = pl.ds((block + 1) * WIDTH, PANEL - (block + 1) * WIDTH)
                current = d_ref[below, here]
                if block > 0:
                    current = current - outer(l_ref[below, done], above)
                l_ref[below, here] = outer(current, inverse)

        for block in range(1, BLOCKS):
            for number, (cond, _) in enumerate(children):
                @pl.when(cond)
                def _():
                    copy(block, number).wait_send()


def panel(a, inverse_blocks):
    return pl.pallas_call(
        panel_kernel,
        out_shape=jax.ShapeDtypeStruct(a.shape, F32),
        in_specs=[pl.BlockSpec(memory_space=pltpu.VMEM)] * 2,
        out_specs=pl.BlockSpec(memory_space=pltpu.VMEM),
        scratch_shapes=[
            pltpu.VMEM((PANEL, PANEL), F32),
            pltpu.VMEM((PANEL, PANEL), F32),
            pltpu.SemaphoreType.DMA((4, BLOCKS - 1)),
            pltpu.SemaphoreType.DMA((BLOCKS - 1,)),
            pltpu.SemaphoreType.DMA,
        ],
        compiler_params=pltpu.CompilerParams(collective_id=0, has_side_effects=True, vmem_limit_bytes=24 * 2**20),
        name="panel",
    )(a, inverse_blocks)


CHUNK = 32
STEP = 2


def spread_kernel(f_ref, row_ref, col_ref, recv_z, recv_y, recv_g, send_z, send_y, send_g, own):
    half, z_hi, x, y, z_lo = place()
    side = row_ref.shape[0] // 2
    chunks = side // CHUNK
    tree_z, parent_z, hops_z = z_first_tree(half, z_hi, x, y, z_lo)
    tree_y, parent_y, hops_y = y_first_tree(half, z_hi, x, y, z_lo)
    root = (y == 0) & (z_lo == 0)
    lead, near = half == y // 2, z_hi == y % 2
    source = lead & near & (x == z_lo)
    column = [
        device(half, 1 - z_hi, x, y, z_lo),
        device(half, z_hi, (x + 1) % 4, y, z_lo),
        device(half, z_hi, (x + 3) % 4, y, z_lo),
        device(1 - half, z_hi, x, y, z_lo),
    ]
    barrier = pltpu.get_barrier_semaphore()

    @pl.when(jnp.logical_not(root))
    def _():
        pl.semaphore_signal(barrier, inc=1, device_id=parent_z, device_id_type=MESH)
        pl.semaphore_signal(barrier, inc=1, device_id=parent_y, device_id_type=MESH)

    for target in column:
        pl.semaphore_signal(barrier, inc=1, device_id=target, device_id_type=MESH)

    @pl.when(root)
    def _():
        mine = pltpu.make_async_copy(f_ref, row_ref, own)
        mine.start()
        mine.wait()

    pl.semaphore_wait(barrier, count(tree_z) + count(tree_y) + len(column))

    def rows(number):
        return pl.ds(pl.multiple_of(number * CHUNK, CHUNK), CHUNK)

    def forward(src, dst, number, tree, sends, recv):
        for slot, (cond, target) in enumerate(tree):
            @pl.when(cond)
            def _():
                remote(src.at[rows(number)], dst.at[rows(number)], sends(slot), recv, target).start()

    def turn(away):
        return jnp.where(away == 3, 1, away)

    def column_tree(bridge):
        from_source = (x - z_lo + 4) % 4
        away = jnp.where(near, from_source, (from_source - bridge + 4) % 4)
        children = [
            (lead & near & (from_source == bridge), column[0]),
            (lead & (away <= 1), column[1]),
            (lead & (away == 0), column[2]),
            (lead, column[3]),
        ]
        hops = turn(away) + jnp.where(lead, 0, 1) + jnp.where(near, 0, 2 + turn(bridge))
        return children, hops

    def along_row(number, offset, tree, sends, recv):
        @pl.when((number >= 0) & (number < chunks))
        def _():
            @pl.when(jnp.logical_not(root))
            def _():
                at = row_ref.at[rows(offset + number)]
                remote(at, at, sends.at[0], recv.at[number], tree[0][1]).wait_recv()

            forward(row_ref, row_ref, offset + number, tree, lambda slot: sends.at[slot], recv.at[number])

            @pl.when(source)
            def _():
                along = offset + number
                forward(row_ref, col_ref, along, column_tree(number % 4)[0], lambda slot: send_g.at[slot, along], recv_g.at[along])

    def along_col(step, offset):
        def one(bridge, carry):
            children, hops = column_tree(bridge)
            number = step - hops * STEP

            @pl.when((number >= 0) & (number < chunks) & (number % 4 == bridge) & jnp.logical_not(source))
            def _():
                along = offset + number
                at = col_ref.at[rows(along)]
                remote(at, at, send_g.at[0, along], recv_g.at[along], column[0]).wait_recv()
                forward(col_ref, col_ref, along, children, lambda slot: send_g.at[slot, along], recv_g.at[along])

            return carry

        lax.fori_loop(0, 4, one, 0)

    start_z, start_y = hops_z * STEP, hops_y * STEP

    def body(step, carry):
        along_row(step - start_z, 0, tree_z, send_z, recv_z)
        along_row(step - start_y, chunks, tree_y, send_y, recv_y)
        along_col(step - start_z, 0)
        along_col(step - start_y, chunks)
        return carry

    lax.fori_loop(0, chunks + STEP * 13, body, 0)

    @pl.when(source)
    def _():
        mine = pltpu.make_async_copy(row_ref, col_ref, own)
        mine.start()
        mine.wait()

    def drain(tree, sends):
        at = row_ref.at[pl.ds(0, side)]
        for slot, (cond, target) in enumerate(tree):
            @pl.when(cond)
            def _():
                remote(at, at, sends.at[slot], recv_z.at[0], target).wait_send()

    drain(tree_z, send_z)
    drain(tree_y, send_y)

    def drain_column(number, carry):
        at = row_ref.at[rows(number)]
        for slot, (cond, target) in enumerate(column_tree(number % 4)[0]):
            @pl.when(cond)
            def _():
                remote(at, at, send_g.at[slot, number], recv_z.at[0], target).wait_send()

        return carry

    lax.fori_loop(0, 2 * chunks, drain_column, 0)


def spread(f):
    chunks = f.shape[0] // 2 // CHUNK
    return pl.pallas_call(
        spread_kernel,
        out_shape=[jax.ShapeDtypeStruct(f.shape, F32)] * 2,
        in_specs=[pl.BlockSpec(memory_space=pltpu.VMEM)],
        out_specs=[pl.BlockSpec(memory_space=pltpu.VMEM)] * 2,
        scratch_shapes=[
            pltpu.SemaphoreType.DMA((chunks,)),
            pltpu.SemaphoreType.DMA((chunks,)),
            pltpu.SemaphoreType.DMA((2 * chunks,)),
            pltpu.SemaphoreType.DMA((4,)),
            pltpu.SemaphoreType.DMA((4,)),
            pltpu.SemaphoreType.DMA((4, 2 * chunks)),
            pltpu.SemaphoreType.DMA,
        ],
        compiler_params=pltpu.CompilerParams(collective_id=1, has_side_effects=True, vmem_limit_bytes=24 * 2**20),
        name="spread",
    )(f)


def exchange_kernel(
    x_ref, parent_ref, maps_ref, out_ref, panel_ref,
    col_ref, row_land_ref, col_land_ref, upper, held, strained, passed, packed, landed, pick, by_col, parts, by_row, put,
    own, first, ring_sent, ring_got, less_sent, less_got, sent, got, kept,
):
    half, z_hi, x, y, z_lo = place()
    z = z_hi * 4 + z_lo
    mid = held.shape[1] // 2
    tile = 256
    rows_dims = ((1,), (1,))
    up, down = (z + 1) % 8, (z + 7) % 8
    above = device(half, up // 4, x, y, up % 4)
    below = device(half, down // 4, x, y, down % 4)

    def peer(number):
        return device((half + number // 16) % 2, z_hi, (x + number // 4) % 4, (y + number) % 4, z_lo)

    mine = pltpu.make_async_copy(x_ref, held.at[0], own)
    mine.start()
    front = pltpu.make_async_copy(parent_ref, out_ref, first)
    front.start()
    barrier = pltpu.get_barrier_semaphore()
    for target in (above, below):
        pl.semaphore_signal(barrier, inc=1, device_id=target, device_id_type=MESH)

    def greet(number, carry):
        pl.semaphore_signal(barrier, inc=1, device_id=peer(number), device_id_type=MESH)
        return carry

    lax.fori_loop(1, 32, greet, 0)
    mine.wait()
    pl.semaphore_wait(barrier, 33)

    def at_of(number):
        return jnp.where(number % 2 == 1, 8 - (number + 1) // 2, number // 2)

    def spot(at):
        return at - at // 7 * 3

    def part(at, side):
        return held.at[spot(at), pl.ds(side * mid, mid), :]


    def ring(at, way, side):
        to = (at + 7) % 8 if way == 0 else (at + 1) % 8
        return remote(
            part(at, side), part(to, side), ring_sent.at[way, at, side], ring_got.at[to, side], (above, below)[way]
        )

    def arrived(at, side):
        remote(part(at, side), part(at, side), ring_sent.at[0, at, side], ring_got.at[at, side], above).wait_recv()

    def less(place, way):
        return remote(
            passed.at[place], strained.at[place], less_sent.at[place], less_got.at[place], (above, below)[way]
        )

    def columns_of(which, at, here):
        slots = lax.broadcasted_iota(jnp.int32, (4 * CAP, SUB), 0)
        col_pick = (slots == col_ref[which, (z + at) % 4]).astype(F32).astype(BF16)
        high, low = split(held[spot(at), here, :])
        return dot(col_pick, high, rows_dims), dot(col_pick, low, rows_dims)

    def strain(at, side, way, place):
        high, low = columns_of(1 + way, at, pl.ds(side * mid, mid))
        passed[place] = high + low
        less(place, way).start()

    def message(number, to):
        to_half, to_x, to_y = (half + to // 16) % 2, (x + to // 4) % 4, (y + to) % 4
        src = packed.at[
            number % 4,
            pl.ds(pl.multiple_of(to_y * CAP, CAP), CAP),
            pl.ds(pl.multiple_of((to_half * 4 + to_x) * 128, 128), 128),
        ]
        dst = landed.at[
            at_of(number), half, pl.ds(pl.multiple_of(y * CAP, CAP), CAP), pl.ds(pl.multiple_of(x * 128, 128), 128)
        ]
        return src, dst

    def deliver(number):
        src, dst = message(number, 0)
        pltpu.make_async_copy(src, dst, kept.at[number]).start()

        def one(to, carry):
            src, dst = message(number, to)
            remote(src, dst, sent.at[number], got.at[number], peer(to)).start()
            return carry

        lax.fori_loop(1, 32, one, 0)

    def others():
        return out_ref.at[pl.ds(0, 31 * 8), :]

    def gone(number):
        remote(others(), others(), sent.at[number], got.at[number], above).wait_send()

    def landed_all(number):
        remote(others(), others(), sent.at[number], got.at[number], above).wait_recv()
        src, dst = message(number, 0)
        pltpu.make_async_copy(src, dst, kept.at[number]).wait()

    def pack(number):
        at = at_of(number)
        there = (z + at) % 8
        for side in range(2):
            lanes = pl.ds(side * mid, mid)
            full = (at != 4) & (at != (3, 5)[side])

            @pl.when(full)
            def _():
                high, low = columns_of(0, at, lanes)
                by_col[: 4 * CAP, lanes] = high.astype(BF16)
                by_col[4 * CAP :, lanes] = low.astype(BF16)

            @pl.when(jnp.logical_not(full))
            def _():
                high, low = split(strained[jnp.where(at == 4, 2 + side, 1 - side)])
                by_col[: 4 * CAP, lanes] = high
                by_col[4 * CAP :, lanes] = low

        def rows(step, carry):
            here = pl.ds(pl.multiple_of(step * tile, tile), tile)
            both = dot(by_col[...], pick[there // 4, here, :], rows_dims)
            packed[number % 4, :, here] = both[: 4 * CAP] + both[4 * CAP :]
            return carry

        lax.fori_loop(0, LOC // tile, rows, 0)

    def rows_of(number, child, step):
        source = (z + at_of(number)) % 8 // 4
        places = lax.broadcasted_iota(jnp.int32, (tile, SUB), 0) + step * tile
        row_put = (places == row_land_ref[child, source]).astype(F32).astype(BF16)
        return dot(row_put, parts[child], rows_dims).astype(BF16)

    def take(number):
        landed_all(number)
        for child in range(2):
            high, low = split(landed[at_of(number), child])
            parts[child, : 4 * CAP] = high
            parts[child, 4 * CAP :] = low

    def unpack_first(number):
        take(number)

        def rows(step, carry):
            here = pl.ds(pl.multiple_of(step * tile, tile), tile)
            for child in range(2):
                by_row[at_of(number) % 4, child, here, :] = rows_of(number, child, step)
            return carry

        lax.fori_loop(0, LOC // tile, rows, 0)

    def unpack_second(number, carry):
        source = (z + at_of(number)) % 4
        for child in range(2):
            places = lax.broadcasted_iota(jnp.int32, (LOC, 4 * CAP), 0)
            col_put = (places == col_land_ref[child, source]).astype(F32).astype(BF16)
            put[child, :, : 4 * CAP] = col_put
            put[child, :, 4 * CAP :] = col_put
        take(number)

        def rows(step, carry):
            here = pl.ds(pl.multiple_of(step * tile, tile), tile)
            total = out_ref[here, :]
            for child in range(2):
                both = by_row[at_of(number) % 4, child, here, :] + rows_of(number, child, step)
                total = total + dot(both, put[child], rows_dims)
            out_ref[here, :] = total
            panel_ref[here, :] = total[:, :PANEL]
            return carry

        lax.fori_loop(0, LOC // tile, rows, 0)
        return carry

    for turn in range(2):
        for way in range(2):
            ring(0, way, (turn + way) % 2).start()
    upper[...] = (
        lax.broadcasted_iota(jnp.int32, (SUB, SUB), 0) < lax.broadcasted_iota(jnp.int32, (SUB, SUB), 1)
    ).astype(F32).astype(BF16)

    def before(member):
        return dot(member.astype(F32).astype(BF16), upper[...], ((1,), (0,)))

    def entries(block):
        return maps_ref[pl.ds(half, 1), pl.ds(pl.multiple_of(block * SUB, SUB), SUB)]

    def send_slots(parents):
        targets = parents >> 10
        member = targets == lax.broadcasted_iota(jnp.int32, (GROUPS, SUB), 0)
        rank = jnp.sum(jnp.where(member, before(member), 0.0), axis=0, keepdims=True)
        return targets, rank.astype(jnp.int32)

    for source in range(2):
        for sub in range(2):
            targets, rank = send_slots(entries(source * 8 + x * 2 + sub))
            slot = (((targets >> 3) * 4 + (targets & 3)) * 2 + sub) * CAP + rank
            slot = jnp.where(((targets >> 2) & 1) == z_hi, slot, -1)
            slots = lax.broadcasted_iota(jnp.int32, (LOC, SUB), 0)
            pick[source, :, sub * SUB : (sub + 1) * SUB] = (slots == slot).astype(F32).astype(BF16)
    for source in range(4):
        targets, rank = send_slots(entries(y * 4 + source))
        for which, stop in enumerate((0, 1, 3)):
            slot = (targets >> 2) * CAP + rank
            col_ref[which, source] = jnp.where((targets & 3) == (z_lo + stop) % 4, slot, -1)

    def landing(child, mine, store):
        parents = jnp.concatenate(
            [maps_ref[child : child + 1, block * SUB : (block + 1) * SUB] for block in range(GROUPS)], axis=0
        )
        member = (parents >> 10) == mine
        rank = jnp.where(member, before(member).astype(jnp.int32), -1)
        place = (parents & (LOC - 1)) + 1
        slots = lax.broadcasted_iota(jnp.int32, (2 * CAP, SUB), 0)
        line = lax.broadcasted_iota(jnp.int32, (8, SUB), 0)

        def side(block, shift):
            values = place[block : block + 1]
            values = jnp.where(line == 0, values >> 5, jnp.where(line == 1, values & 31, 0)).astype(F32).astype(BF16)
            mine_rank = rank[block : block + 1]
            hit = slots == jnp.where(mine_rank < 0, -1, mine_rank + shift)
            return dot(values, hit.astype(F32).astype(BF16), rows_dims)

        store(lambda first, second: (lambda both: (both[0:1] * 32.0 + both[1:2]).astype(jnp.int32) - 1)(
            side(first, 0) + side(second, CAP)
        ))

    for child in range(2):
        def rows_land(pair):
            for source in range(2):
                for at_x in range(4):
                    block = source * 8 + at_x * 2
                    row_land_ref[child, source, :, at_x * 128 : (at_x + 1) * 128] = pair(block, block + 1)

        def cols_land(pair):
            for source in range(4):
                for at_y in range(2):
                    col_land_ref[child, source, :, at_y * 128 : (at_y + 1) * 128] = pair(
                        at_y * 8 + source, at_y * 8 + 4 + source
                    )

        landing(child, half * 8 + z_hi * 4 + x, rows_land)
        landing(child, y * 4 + z_lo, cols_land)
    front.wait()

    def event(number, carry):
        @pl.when(number == 1)
        def _():
            for turn in range(2):
                for way in range(2):
                    at, side = (7, 1)[way], (turn + way) % 2
                    arrived(at, side)
                    ring(at, way, side).start()

        @pl.when(number == 3)
        def _():
            for way in range(2):
                at, side = (6, 2)[way], way
                arrived(at, side)
                ring(at, way, side).start()
            for way in range(2):
                at, side = (6, 2)[way], 1 - way
                arrived(at, side)
                strain(at, side, way, way)

        @pl.when(number == 5)
        def _():
            for way in range(2):
                at, side = (5, 3)[way], way
                arrived(at, side)
                strain(at, side, way, 2 + way)
            for way in range(2):
                less(way, way).wait_recv()

        @pl.when(number == 7)
        def _():
            for way in range(2):
                less(2 + way, way).wait_recv()

        @pl.when(number >= 4)
        def _():
            gone(number - 4)

        pack(number)

        @pl.when((number >= 3) & (number < 7))
        def _():
            unpack_first(number - 3)

        deliver(number)
        return carry

    lax.fori_loop(0, 8, event, 0)
    lax.fori_loop(4, 8, unpack_second, 0)

    def settle(number, carry):
        gone(number)
        return carry

    lax.fori_loop(4, 8, settle, 0)
    for way in range(2):
        for at in ((0, 7), (0, 1))[way]:
            for side in range(2):
                ring(at, way, side).wait_send()
        ring((6, 2)[way], way, way).wait_send()
        less(way, way).wait_send()
        less(2 + way, way).wait_send()


def exchange(block, parent, maps):
    rows, cols = block.shape
    return pl.pallas_call(
        exchange_kernel,
        out_shape=[jax.ShapeDtypeStruct(parent.shape, F32), jax.ShapeDtypeStruct((LOC, PANEL), F32)],
        in_specs=[pl.BlockSpec(memory_space=pl.ANY)] * 2 + [pl.BlockSpec(memory_space=pltpu.VMEM)],
        out_specs=[pl.BlockSpec(memory_space=pltpu.VMEM)] * 2,
        scratch_shapes=[
            pltpu.VMEM((3, 4, 1, SUB), jnp.int32),
            pltpu.VMEM((2, 2, 1, SUB), jnp.int32),
            pltpu.VMEM((2, 4, 1, 4 * CAP), jnp.int32),
            pltpu.VMEM((SUB, SUB), BF16),
            pltpu.VMEM((7, rows, cols), F32),
            pltpu.VMEM((4, 4 * CAP, SUB), F32),
            pltpu.VMEM((4, 4 * CAP, SUB), F32),
            pltpu.VMEM((4, 4 * CAP, LOC), F32),
            pltpu.VMEM((8, 2, 4 * CAP, SUB), F32),
            pltpu.VMEM((2, LOC, rows), BF16),
            pltpu.VMEM((8 * CAP, LOC), BF16),
            pltpu.VMEM((2, 8 * CAP, SUB), BF16),
            pltpu.VMEM((4, 2, LOC, 8 * CAP), BF16),
            pltpu.VMEM((2, LOC, 8 * CAP), BF16),
            pltpu.SemaphoreType.DMA,
            pltpu.SemaphoreType.DMA,
            pltpu.SemaphoreType.DMA((2, 8, 2)),
            pltpu.SemaphoreType.DMA((8, 2)),
            pltpu.SemaphoreType.DMA((4,)),
            pltpu.SemaphoreType.DMA((4,)),
            pltpu.SemaphoreType.DMA((8,)),
            pltpu.SemaphoreType.DMA((8,)),
            pltpu.SemaphoreType.DMA((8,)),
        ],
        compiler_params=pltpu.CompilerParams(collective_id=2, has_side_effects=True, vmem_limit_bytes=63 * 2**20),
        name="exchange",
    )(block, parent, maps)


def local(parent_front, child_blocks, row_maps, inverse_blocks):
    assembled, columns = exchange(child_blocks[0], parent_front, row_maps)
    factor = panel(columns, inverse_blocks)
    factor_rows, factor_cols = spread(factor)
    product = lax.dot_general(
        factor_rows, factor_cols, (((1,), (1,)), ((), ())), precision=lax.Precision.HIGH, preferred_element_type=F32
    )
    return assembled - product, factor_rows.astype(BF16)


def solution(mesh):
    in_specs = (P(("half", "row"), "col"), P("half", "row", "col"), P(), P())
    out_specs = (P(("half", "row"), "col"), P(("half", "row"), None))
    return jax.shard_map(local, mesh=mesh, in_specs=in_specs, out_specs=out_specs, check_vma=False)
```

```python
import functools

import jax
import jax.numpy as jnp
from jax import lax
from jax.experimental import pallas as pl
from jax.experimental.pallas import tpu as pltpu
from jax.sharding import PartitionSpec as P

MESH = pl.DeviceIdType.MESH
F32 = jnp.float32
BF16 = jnp.bfloat16

SUB = 512
CAP = 64
LOC = 1024
GROUPS = 16
WIDTH = 128
BLOCKS = 4
PANEL = WIDTH * BLOCKS


def dot(left, right, dims):
    return lax.dot_general(left, right, (dims, ((), ())), preferred_element_type=F32)


def place():
    half, row, col = lax.axis_index("half"), lax.axis_index("row"), lax.axis_index("col")
    return half, row // 4, row % 4, col // 4, col % 4


def device(half, z_hi, x, y, z_lo):
    return {"half": half, "row": z_hi * 4 + x, "col": y * 4 + z_lo}


def group_tree(half, z_hi, x, y, z_lo, src_half, src_z, src_x):
    away = (x - src_x + 4) % 4
    lead = half == src_half
    source = lead & (z_hi == src_z) & (away == 0)
    children = [
        (source, device(half, 1 - z_hi, x, y, z_lo)),
        (lead & (away <= 1), device(half, z_hi, (x + 1) % 4, y, z_lo)),
        (lead & (away == 0), device(half, z_hi, (x + 3) % 4, y, z_lo)),
        (lead, device(1 - half, z_hi, x, y, z_lo)),
    ]
    up_x = jnp.where(away == 3, (x + 1) % 4, (x + 3) % 4)
    parent_half = jnp.where(lead, half, 1 - half)
    parent_z = jnp.where(lead & (away == 0), 1 - z_hi, z_hi)
    parent_x = jnp.where(lead & (away != 0), up_x, x)
    parent = device(parent_half, parent_z, parent_x, y, z_lo)
    hops = jnp.where(away == 3, 1, away) + jnp.where(lead, 0, 1) + jnp.where(z_hi == src_z, 0, 2)
    return source, children, parent, hops


def z_first_tree(half, z_hi, x, y, z_lo):
    at = lambda y2, z2: device(half, z_hi, x, y2, z2)
    children = [
        ((y == 0) & (z_lo < 3), at(0, z_lo + 1)),
        ((y <= 1) & (z_lo >= 1), at(y + 1, z_lo)),
        ((y == 0) & (z_lo >= 1), at(3, z_lo)),
        ((y >= 1) & (z_lo == 1), at(y, 0)),
    ]
    back = (z_lo == 0) & (y >= 1)
    parent_y = jnp.where(back, y, jnp.where(y == 2, 1, 0))
    parent_z = jnp.where(back, 1, jnp.where(y == 0, z_lo - 1, z_lo))
    turn = jnp.where(y == 3, 1, y)
    hops = jnp.where(back, turn + 2, turn + z_lo)
    return children, at(parent_y, parent_z), hops


def y_first_tree(half, z_hi, x, y, z_lo):
    at = lambda y2, z2: device(half, z_hi, x, y2, z2)
    children = [
        ((z_lo == 0) & (y <= 1), at(y + 1, 0)),
        ((z_lo == 0) & (y == 0), at(3, 0)),
        ((y >= 1) & (z_lo < 3), at(y, z_lo + 1)),
        ((y == 1) & (z_lo >= 1), at(0, z_lo)),
    ]
    back = (y == 0) & (z_lo >= 1)
    parent_y = jnp.where(z_lo == 0, jnp.where(y == 2, 1, 0), jnp.where(y == 0, 1, y))
    parent_z = jnp.where((z_lo == 0) | back, z_lo, z_lo - 1)
    turn = jnp.where(y == 3, 1, y)
    hops = jnp.where(back, z_lo + 2, turn + z_lo)
    return children, at(parent_y, parent_z), hops


def count(children):
    total = 0
    for cond, _ in children:
        total = total + cond.astype(jnp.int32)
    return total


def wait_for(barrier, signals):
    @pl.when(signals > 0)
    def _():
        pl.semaphore_wait(barrier, signals)


def remote(src, dst, send, recv, target):
    return pltpu.make_async_remote_copy(
        src_ref=src, dst_ref=dst, send_sem=send, recv_sem=recv, device_id=target, device_id_type=MESH
    )


def split(value):
    high = value.astype(BF16)
    return high, (value - high.astype(F32)).astype(BF16)


def outer(left, right):
    left_high, left_low = split(left)
    right_high, right_low = split(right)
    dims = ((1,), (1,))
    return dot(left_high, right_high, dims) + (dot(left_high, right_low, dims) + dot(left_low, right_high, dims))


def panel_kernel(a_ref, inv_ref, f_ref, d_ref, l_ref, send, recv, own):
    half, z_hi, x, y, z_lo = place()
    source, children, parent, _ = group_tree(half, z_hi, x, y, z_lo, 0, 0, 0)
    active = (y == 0) & (z_lo == 0)
    barrier = pltpu.get_barrier_semaphore()

    @pl.when(active)
    def _():
        @pl.when(jnp.logical_not(source))
        def _():
            pl.semaphore_signal(barrier, inc=1, device_id=parent, device_id_type=MESH)

        wait_for(barrier, count(children))

        def piece(ref, block):
            return ref.at[pl.ds(block * WIDTH, WIDTH), pl.ds(0, block * WIDTH)]

        def copy(block, number, src=d_ref):
            return remote(
                piece(src, block), piece(d_ref, block), send.at[number, block - 1], recv.at[block - 1], children[number][1]
            )

        def mine(block):
            return pltpu.make_async_copy(piece(a_ref, block), piece(d_ref, block), own.at[block - 1])

        @pl.when(source)
        def _():
            for block in range(1, BLOCKS):
                for number in range(len(children)):
                    copy(block, number, a_ref).start()
                mine(block).start()

        lower = lax.broadcasted_iota(jnp.int32, (WIDTH, WIDTH), 0) >= lax.broadcasted_iota(jnp.int32, (WIDTH, WIDTH), 1)
        f_ref[:, :WIDTH] = outer(a_ref[:, :WIDTH], jnp.where(lower, inv_ref[0], 0.0))

        @pl.when(source)
        def _():
            for block in range(1, BLOCKS):
                mine(block).wait()

        @pl.when(jnp.logical_not(source))
        def _():
            for block in range(1, BLOCKS):
                copy(block, 0).wait_recv()
                for number, (cond, _) in enumerate(children):
                    @pl.when(cond)
                    def _():
                        copy(block, number).start()

        for block in range(BLOCKS):
            inverse = jnp.where(lower, inv_ref[block], 0.0)
            here = pl.ds(block * WIDTH, WIDTH)
            done = pl.ds(0, block * WIDTH)
            if block > 0:
                above = l_ref[here, done]
                f_ref[:, here] = outer(a_ref[:, here] - outer(f_ref[:, done], above), inverse)
            if block + 1 < BLOCKS:
                below = pl.ds((block + 1) * WIDTH, PANEL - (block + 1) * WIDTH)
                current = d_ref[below, here]
                if block > 0:
                    current = current - outer(l_ref[below, done], above)
                l_ref[below, here] = outer(current, inverse)

        for block in range(1, BLOCKS):
            for number, (cond, _) in enumerate(children):
                @pl.when(cond)
                def _():
                    copy(block, number).wait_send()


def panel(a, inverse_blocks):
    return pl.pallas_call(
        panel_kernel,
        out_shape=jax.ShapeDtypeStruct(a.shape, F32),
        in_specs=[pl.BlockSpec(memory_space=pltpu.VMEM)] * 2,
        out_specs=pl.BlockSpec(memory_space=pltpu.VMEM),
        scratch_shapes=[
            pltpu.VMEM((PANEL, PANEL), F32),
            pltpu.VMEM((PANEL, PANEL), F32),
            pltpu.SemaphoreType.DMA((4, BLOCKS - 1)),
            pltpu.SemaphoreType.DMA((BLOCKS - 1,)),
            pltpu.SemaphoreType.DMA((BLOCKS - 1,)),
        ],
        compiler_params=pltpu.CompilerParams(collective_id=0, has_side_effects=True, vmem_limit_bytes=24 * 2**20),
        name="panel",
    )(a, inverse_blocks)


CHUNK = 32
STEP = 2


def spread_kernel(f_ref, row_ref, col_ref, recv_z, recv_y, recv_g, send_z, send_y, send_g, own):
    half, z_hi, x, y, z_lo = place()
    side = row_ref.shape[0] // 2
    chunks = side // CHUNK
    tree_z, parent_z, hops_z = z_first_tree(half, z_hi, x, y, z_lo)
    tree_y, parent_y, hops_y = y_first_tree(half, z_hi, x, y, z_lo)
    root = (y == 0) & (z_lo == 0)
    lead, near = half == y // 2, z_hi == y % 2
    source = lead & near & (x == z_lo)
    column = [
        device(half, 1 - z_hi, x, y, z_lo),
        device(half, z_hi, (x + 1) % 4, y, z_lo),
        device(half, z_hi, (x + 3) % 4, y, z_lo),
        device(1 - half, z_hi, x, y, z_lo),
    ]
    barrier = pltpu.get_barrier_semaphore()

    @pl.when(jnp.logical_not(root))
    def _():
        pl.semaphore_signal(barrier, inc=1, device_id=parent_z, device_id_type=MESH)
        pl.semaphore_signal(barrier, inc=1, device_id=parent_y, device_id_type=MESH)

    for target in column:
        pl.semaphore_signal(barrier, inc=1, device_id=target, device_id_type=MESH)

    @pl.when(root)
    def _():
        mine = pltpu.make_async_copy(f_ref, row_ref, own)
        mine.start()
        mine.wait()

    pl.semaphore_wait(barrier, count(tree_z) + count(tree_y) + len(column))

    def rows(number):
        return pl.ds(pl.multiple_of(number * CHUNK, CHUNK), CHUNK)

    def forward(src, dst, number, tree, sends, recv):
        for slot, (cond, target) in enumerate(tree):
            @pl.when(cond)
            def _():
                remote(src.at[rows(number)], dst.at[rows(number)], sends(slot), recv, target).start()

    def turn(away):
        return jnp.where(away == 3, 1, away)

    def column_tree(bridge):
        from_source = (x - z_lo + 4) % 4
        away = jnp.where(near, from_source, (from_source - bridge + 4) % 4)
        children = [
            (lead & near & (from_source == bridge), column[0]),
            (lead & (away <= 1), column[1]),
            (lead & (away == 0), column[2]),
            (lead, column[3]),
        ]
        hops = turn(away) + jnp.where(lead, 0, 1) + jnp.where(near, 0, 2 + turn(bridge))
        return children, hops

    def along_row(number, offset, tree, sends, recv):
        @pl.when((number >= 0) & (number < chunks))
        def _():
            @pl.when(jnp.logical_not(root))
            def _():
                at = row_ref.at[rows(offset + number)]
                remote(at, at, sends.at[0], recv.at[number], tree[0][1]).wait_recv()

            forward(row_ref, row_ref, offset + number, tree, lambda slot: sends.at[slot], recv.at[number])

            @pl.when(source)
            def _():
                along = offset + number
                forward(row_ref, col_ref, along, column_tree(number % 4)[0], lambda slot: send_g.at[slot, along], recv_g.at[along])

    def along_col(step, offset):
        def one(bridge, carry):
            children, hops = column_tree(bridge)
            number = step - hops * STEP

            @pl.when((number >= 0) & (number < chunks) & (number % 4 == bridge) & jnp.logical_not(source))
            def _():
                along = offset + number
                at = col_ref.at[rows(along)]
                remote(at, at, send_g.at[0, along], recv_g.at[along], column[0]).wait_recv()
                forward(col_ref, col_ref, along, children, lambda slot: send_g.at[slot, along], recv_g.at[along])

            return carry

        lax.fori_loop(0, 4, one, 0)

    start_z, start_y = hops_z * STEP, hops_y * STEP

    def body(step, carry):
        along_row(step - start_z, 0, tree_z, send_z, recv_z)
        along_row(step - start_y, chunks, tree_y, send_y, recv_y)
        along_col(step - start_z, 0)
        along_col(step - start_y, chunks)
        return carry

    lax.fori_loop(0, chunks + STEP * 13, body, 0)

    @pl.when(source)
    def _():
        mine = pltpu.make_async_copy(row_ref, col_ref, own)
        mine.start()
        mine.wait()

    def drain(tree, sends):
        at = row_ref.at[pl.ds(0, side)]
        for slot, (cond, target) in enumerate(tree):
            @pl.when(cond)
            def _():
                remote(at, at, sends.at[slot], recv_z.at[0], target).wait_send()

    drain(tree_z, send_z)
    drain(tree_y, send_y)

    def drain_column(number, carry):
        at = row_ref.at[rows(number)]
        for slot, (cond, target) in enumerate(column_tree(number % 4)[0]):
            @pl.when(cond)
            def _():
                remote(at, at, send_g.at[slot, number], recv_z.at[0], target).wait_send()

        return carry

    lax.fori_loop(0, 2 * chunks, drain_column, 0)


def spread(f):
    chunks = f.shape[0] // 2 // CHUNK
    return pl.pallas_call(
        spread_kernel,
        out_shape=[jax.ShapeDtypeStruct(f.shape, F32)] * 2,
        in_specs=[pl.BlockSpec(memory_space=pltpu.VMEM)],
        out_specs=[pl.BlockSpec(memory_space=pltpu.VMEM)] * 2,
        scratch_shapes=[
            pltpu.SemaphoreType.DMA((chunks,)),
            pltpu.SemaphoreType.DMA((chunks,)),
            pltpu.SemaphoreType.DMA((2 * chunks,)),
            pltpu.SemaphoreType.DMA((4,)),
            pltpu.SemaphoreType.DMA((4,)),
            pltpu.SemaphoreType.DMA((4, 2 * chunks)),
            pltpu.SemaphoreType.DMA,
        ],
        compiler_params=pltpu.CompilerParams(collective_id=1, has_side_effects=True, vmem_limit_bytes=24 * 2**20),
        name="spread",
    )(f)


def exchange_kernel(
    x_ref, parent_ref, maps_ref, out_ref, panel_ref,
    col_ref, row_land_ref, col_land_ref, upper, held, strained, passed, packed, landed, pick, by_col, parts, by_row, put,
    own, first, ring_sent, ring_got, less_sent, less_got, sent, got, kept,
):
    half, z_hi, x, y, z_lo = place()
    z = z_hi * 4 + z_lo
    mid = held.shape[1] // 2
    tile = 256
    rows_dims = ((1,), (1,))
    up, down = (z + 1) % 8, (z + 7) % 8
    above = device(half, up // 4, x, y, up % 4)
    below = device(half, down // 4, x, y, down % 4)

    def peer(number):
        return device((half + number // 16) % 2, z_hi, (x + number // 4) % 4, (y + number) % 4, z_lo)

    mine = pltpu.make_async_copy(x_ref, held.at[0], own)
    mine.start()
    front = pltpu.make_async_copy(parent_ref, out_ref, first)
    front.start()
    barrier = pltpu.get_barrier_semaphore()
    for target in (above, below):
        pl.semaphore_signal(barrier, inc=1, device_id=target, device_id_type=MESH)

    def greet(number, carry):
        pl.semaphore_signal(barrier, inc=1, device_id=peer(number), device_id_type=MESH)
        return carry

    lax.fori_loop(1, 32, greet, 0)
    mine.wait()
    pl.semaphore_wait(barrier, 33)

    def at_of(number):
        return jnp.where(number % 2 == 1, 8 - (number + 1) // 2, number // 2)

    def spot(at):
        return at - at // 7 * 3

    def part(at, side):
        return held.at[spot(at), pl.ds(side * mid, mid), :]


    def ring(at, way, side):
        to = (at + 7) % 8 if way == 0 else (at + 1) % 8
        return remote(
            part(at, side), part(to, side), ring_sent.at[way, at, side], ring_got.at[to, side], (above, below)[way]
        )

    def arrived(at, side):
        remote(part(at, side), part(at, side), ring_sent.at[0, at, side], ring_got.at[at, side], above).wait_recv()

    def less(place, way):
        return remote(
            passed.at[place], strained.at[place], less_sent.at[place], less_got.at[place], (above, below)[way]
        )

    def columns_of(which, at, here):
        slots = lax.broadcasted_iota(jnp.int32, (4 * CAP, SUB), 0)
        col_pick = (slots == col_ref[which, (z + at) % 4]).astype(F32).astype(BF16)
        high, low = split(held[spot(at), here, :])
        return dot(col_pick, high, rows_dims), dot(col_pick, low, rows_dims)

    def strain(at, side, way, place):
        high, low = columns_of(1 + way, at, pl.ds(side * mid, mid))
        passed[place] = high + low
        less(place, way).start()

    def message(number, to):
        to_half, to_x, to_y = (half + to // 16) % 2, (x + to // 4) % 4, (y + to) % 4
        src = packed.at[
            number % 4,
            pl.ds(pl.multiple_of(to_y * CAP, CAP), CAP),
            pl.ds(pl.multiple_of((to_half * 4 + to_x) * 128, 128), 128),
        ]
        dst = landed.at[
            at_of(number), half, pl.ds(pl.multiple_of(y * CAP, CAP), CAP), pl.ds(pl.multiple_of(x * 128, 128), 128)
        ]
        return src, dst

    def deliver(number):
        src, dst = message(number, 0)
        pltpu.make_async_copy(src, dst, kept.at[number]).start()

        def one(to, carry):
            src, dst = message(number, to)
            remote(src, dst, sent.at[number], got.at[number], peer(to)).start()
            return carry

        lax.fori_loop(1, 32, one, 0)

    def others():
        return out_ref.at[pl.ds(0, 31 * 8), :]

    def gone(number):
        remote(others(), others(), sent.at[number], got.at[number], above).wait_send()

    def landed_all(number):
        remote(others(), others(), sent.at[number], got.at[number], above).wait_recv()
        src, dst = message(number, 0)
        pltpu.make_async_copy(src, dst, kept.at[number]).wait()

    def pack(number):
        at = at_of(number)
        there = (z + at) % 8
        for side in range(2):
            lanes = pl.ds(side * mid, mid)
            full = (at != 4) & (at != (3, 5)[side])

            @pl.when(full)
            def _():
                high, low = columns_of(0, at, lanes)
                by_col[: 4 * CAP, lanes] = high.astype(BF16)
                by_col[4 * CAP :, lanes] = low.astype(BF16)

            @pl.when(jnp.logical_not(full))
            def _():
                high, low = split(strained[jnp.where(at == 4, 2 + side, 1 - side)])
                by_col[: 4 * CAP, lanes] = high
                by_col[4 * CAP :, lanes] = low

        def rows(step, carry):
            here = pl.ds(pl.multiple_of(step * tile, tile), tile)
            both = dot(by_col[...], pick[there // 4, here, :], rows_dims)
            packed[number % 4, :, here] = both[: 4 * CAP] + both[4 * CAP :]
            return carry

        lax.fori_loop(0, LOC // tile, rows, 0)

    def rows_of(number, child, step):
        source = (z + at_of(number)) % 8 // 4
        places = lax.broadcasted_iota(jnp.int32, (tile, SUB), 0) + step * tile
        row_put = (places == row_land_ref[child, source]).astype(F32).astype(BF16)
        return dot(row_put, parts[child], rows_dims).astype(BF16)

    def take(number):
        landed_all(number)
        for child in range(2):
            high, low = split(landed[at_of(number), child])
            parts[child, : 4 * CAP] = high
            parts[child, 4 * CAP :] = low

    def unpack_first(number):
        take(number)

        def rows(step, carry):
            here = pl.ds(pl.multiple_of(step * tile, tile), tile)
            for child in range(2):
                by_row[at_of(number) % 4, child, here, :] = rows_of(number, child, step)
            return carry

        lax.fori_loop(0, LOC // tile, rows, 0)

    def unpack_second(number, carry):
        source = (z + at_of(number)) % 4
        for child in range(2):
            places = lax.broadcasted_iota(jnp.int32, (LOC, 4 * CAP), 0)
            col_put = (places == col_land_ref[child, source]).astype(F32).astype(BF16)
            put[child, :, : 4 * CAP] = col_put
            put[child, :, 4 * CAP :] = col_put
        take(number)

        def rows(step, carry):
            here = pl.ds(pl.multiple_of(step * tile, tile), tile)
            total = out_ref[here, :]
            for child in range(2):
                both = by_row[at_of(number) % 4, child, here, :] + rows_of(number, child, step)
                total = total + dot(both, put[child], rows_dims)
            out_ref[here, :] = total
            panel_ref[here, :] = total[:, :PANEL]
            return carry

        lax.fori_loop(0, LOC // tile, rows, 0)
        return carry

    for turn in range(2):
        for way in range(2):
            ring(0, way, (turn + way) % 2).start()
    upper[...] = (
        lax.broadcasted_iota(jnp.int32, (SUB, SUB), 0) < lax.broadcasted_iota(jnp.int32, (SUB, SUB), 1)
    ).astype(F32).astype(BF16)

    def before(member):
        return dot(member.astype(F32).astype(BF16), upper[...], ((1,), (0,)))

    def entries(block):
        return maps_ref[pl.ds(half, 1), pl.ds(pl.multiple_of(block * SUB, SUB), SUB)]

    def send_slots(parents):
        targets = parents >> 10
        member = targets == lax.broadcasted_iota(jnp.int32, (GROUPS, SUB), 0)
        rank = jnp.sum(jnp.where(member, before(member), 0.0), axis=0, keepdims=True)
        return targets, rank.astype(jnp.int32)

    for source in range(2):
        for sub in range(2):
            targets, rank = send_slots(entries(source * 8 + x * 2 + sub))
            slot = (((targets >> 3) * 4 + (targets & 3)) * 2 + sub) * CAP + rank
            slot = jnp.where(((targets >> 2) & 1) == z_hi, slot, -1)
            slots = lax.broadcasted_iota(jnp.int32, (LOC, SUB), 0)
            pick[source, :, sub * SUB : (sub + 1) * SUB] = (slots == slot).astype(F32).astype(BF16)
    for source in range(4):
        targets, rank = send_slots(entries(y * 4 + source))
        for which, stop in enumerate((0, 1, 3)):
            slot = (targets >> 2) * CAP + rank
            col_ref[which, source] = jnp.where((targets & 3) == (z_lo + stop) % 4, slot, -1)

    def landing(child, mine, store):
        parents = jnp.concatenate(
            [maps_ref[child : child + 1, block * SUB : (block + 1) * SUB] for block in range(GROUPS)], axis=0
        )
        member = (parents >> 10) == mine
        rank = jnp.where(member, before(member).astype(jnp.int32), -1)
        place = (parents & (LOC - 1)) + 1
        slots = lax.broadcasted_iota(jnp.int32, (2 * CAP, SUB), 0)
        line = lax.broadcasted_iota(jnp.int32, (8, SUB), 0)

        def side(block, shift):
            values = place[block : block + 1]
            values = jnp.where(line == 0, values >> 5, jnp.where(line == 1, values & 31, 0)).astype(F32).astype(BF16)
            mine_rank = rank[block : block + 1]
            hit = slots == jnp.where(mine_rank < 0, -1, mine_rank + shift)
            return dot(values, hit.astype(F32).astype(BF16), rows_dims)

        store(lambda first, second: (lambda both: (both[0:1] * 32.0 + both[1:2]).astype(jnp.int32) - 1)(
            side(first, 0) + side(second, CAP)
        ))

    for child in range(2):
        def rows_land(pair):
            for source in range(2):
                for at_x in range(4):
                    block = source * 8 + at_x * 2
                    row_land_ref[child, source, :, at_x * 128 : (at_x + 1) * 128] = pair(block, block + 1)

        def cols_land(pair):
            for source in range(4):
                for at_y in range(2):
                    col_land_ref[child, source, :, at_y * 128 : (at_y + 1) * 128] = pair(
                        at_y * 8 + source, at_y * 8 + 4 + source
                    )

        landing(child, half * 8 + z_hi * 4 + x, rows_land)
        landing(child, y * 4 + z_lo, cols_land)
    front.wait()

    def event(number, carry):
        @pl.when(number == 1)
        def _():
            for turn in range(2):
                for way in range(2):
                    at, side = (7, 1)[way], (turn + way) % 2
                    arrived(at, side)
                    ring(at, way, side).start()

        @pl.when(number == 3)
        def _():
            for way in range(2):
                at, side = (6, 2)[way], way
                arrived(at, side)
                ring(at, way, side).start()
            for way in range(2):
                at, side = (6, 2)[way], 1 - way
                arrived(at, side)
                strain(at, side, way, way)

        @pl.when(number == 5)
        def _():
            for way in range(2):
                at, side = (5, 3)[way], way
                arrived(at, side)
                strain(at, side, way, 2 + way)
            for way in range(2):
                less(way, way).wait_recv()

        @pl.when(number == 7)
        def _():
            for way in range(2):
                less(2 + way, way).wait_recv()

        @pl.when(number >= 4)
        def _():
            gone(number - 4)

        pack(number)

        @pl.when((number >= 3) & (number < 7))
        def _():
            unpack_first(number - 3)

        deliver(number)
        return carry

    lax.fori_loop(0, 8, event, 0)
    lax.fori_loop(4, 8, unpack_second, 0)

    def settle(number, carry):
        gone(number)
        return carry

    lax.fori_loop(4, 8, settle, 0)
    for way in range(2):
        for at in ((0, 7), (0, 1))[way]:
            for side in range(2):
                ring(at, way, side).wait_send()
        ring((6, 2)[way], way, way).wait_send()
        less(way, way).wait_send()
        less(2 + way, way).wait_send()


def exchange(block, parent, maps):
    rows, cols = block.shape
    return pl.pallas_call(
        exchange_kernel,
        out_shape=[jax.ShapeDtypeStruct(parent.shape, F32), jax.ShapeDtypeStruct((LOC, PANEL), F32)],
        in_specs=[pl.BlockSpec(memory_space=pl.ANY)] * 2 + [pl.BlockSpec(memory_space=pltpu.VMEM)],
        out_specs=[pl.BlockSpec(memory_space=pltpu.VMEM)] * 2,
        scratch_shapes=[
            pltpu.VMEM((3, 4, 1, SUB), jnp.int32),
            pltpu.VMEM((2, 2, 1, SUB), jnp.int32),
            pltpu.VMEM((2, 4, 1, 4 * CAP), jnp.int32),
            pltpu.VMEM((SUB, SUB), BF16),
            pltpu.VMEM((7, rows, cols), F32),
            pltpu.VMEM((4, 4 * CAP, SUB), F32),
            pltpu.VMEM((4, 4 * CAP, SUB), F32),
            pltpu.VMEM((4, 4 * CAP, LOC), F32),
            pltpu.VMEM((8, 2, 4 * CAP, SUB), F32),
            pltpu.VMEM((2, LOC, rows), BF16),
            pltpu.VMEM((8 * CAP, LOC), BF16),
            pltpu.VMEM((2, 8 * CAP, SUB), BF16),
            pltpu.VMEM((4, 2, LOC, 8 * CAP), BF16),
            pltpu.VMEM((2, LOC, 8 * CAP), BF16),
            pltpu.SemaphoreType.DMA,
            pltpu.SemaphoreType.DMA,
            pltpu.SemaphoreType.DMA((2, 8, 2)),
            pltpu.SemaphoreType.DMA((8, 2)),
            pltpu.SemaphoreType.DMA((4,)),
            pltpu.SemaphoreType.DMA((4,)),
            pltpu.SemaphoreType.DMA((8,)),
            pltpu.SemaphoreType.DMA((8,)),
            pltpu.SemaphoreType.DMA((8,)),
        ],
        compiler_params=pltpu.CompilerParams(collective_id=2, has_side_effects=True, vmem_limit_bytes=63 * 2**20),
        name="exchange",
    )(block, parent, maps)


def local(parent_front, child_blocks, row_maps, inverse_blocks):
    assembled, columns = exchange(child_blocks[0], parent_front, row_maps)
    factor = panel(columns, inverse_blocks)
    factor_rows, factor_cols = spread(factor)
    product = lax.dot_general(
        factor_rows, factor_cols, (((1,), (1,)), ((), ())), precision=lax.Precision.HIGH, preferred_element_type=F32
    )
    return assembled - product, factor_rows.astype(BF16)


def solution(mesh):
    in_specs = (P(("half", "row"), "col"), P("half", "row", "col"), P(), P())
    out_specs = (P(("half", "row"), "col"), P(("half", "row"), None))
    return jax.shard_map(local, mesh=mesh, in_specs=in_specs, out_specs=out_specs, check_vma=False)
```

```python
import functools

import jax
import jax.numpy as jnp
from jax import lax
from jax.experimental import pallas as pl
from jax.experimental.pallas import tpu as pltpu
from jax.sharding import PartitionSpec as P

MESH = pl.DeviceIdType.MESH
F32 = jnp.float32
BF16 = jnp.bfloat16

SUB = 512
CAP = 64
LOC = 1024
GROUPS = 16
WIDTH = 128
BLOCKS = 4
PANEL = WIDTH * BLOCKS


def dot(left, right, dims):
    return lax.dot_general(left, right, (dims, ((), ())), preferred_element_type=F32)


def place():
    half, row, col = lax.axis_index("half"), lax.axis_index("row"), lax.axis_index("col")
    return half, row // 4, row % 4, col // 4, col % 4


def device(half, z_hi, x, y, z_lo):
    return {"half": half, "row": z_hi * 4 + x, "col": y * 4 + z_lo}


def group_tree(half, z_hi, x, y, z_lo, src_half, src_z, src_x):
    away = (x - src_x + 4) % 4
    lead = half == src_half
    source = lead & (z_hi == src_z) & (away == 0)
    children = [
        (source, device(half, 1 - z_hi, x, y, z_lo)),
        (lead & (away <= 1), device(half, z_hi, (x + 1) % 4, y, z_lo)),
        (lead & (away == 0), device(half, z_hi, (x + 3) % 4, y, z_lo)),
        (lead, device(1 - half, z_hi, x, y, z_lo)),
    ]
    up_x = jnp.where(away == 3, (x + 1) % 4, (x + 3) % 4)
    parent_half = jnp.where(lead, half, 1 - half)
    parent_z = jnp.where(lead & (away == 0), 1 - z_hi, z_hi)
    parent_x = jnp.where(lead & (away != 0), up_x, x)
    parent = device(parent_half, parent_z, parent_x, y, z_lo)
    hops = jnp.where(away == 3, 1, away) + jnp.where(lead, 0, 1) + jnp.where(z_hi == src_z, 0, 2)
    return source, children, parent, hops


def z_first_tree(half, z_hi, x, y, z_lo):
    at = lambda y2, z2: device(half, z_hi, x, y2, z2)
    children = [
        ((y == 0) & (z_lo < 3), at(0, z_lo + 1)),
        ((y <= 1) & (z_lo >= 1), at(y + 1, z_lo)),
        ((y == 0) & (z_lo >= 1), at(3, z_lo)),
        ((y >= 1) & (z_lo == 1), at(y, 0)),
    ]
    back = (z_lo == 0) & (y >= 1)
    parent_y = jnp.where(back, y, jnp.where(y == 2, 1, 0))
    parent_z = jnp.where(back, 1, jnp.where(y == 0, z_lo - 1, z_lo))
    turn = jnp.where(y == 3, 1, y)
    hops = jnp.where(back, turn + 2, turn + z_lo)
    return children, at(parent_y, parent_z), hops


def y_first_tree(half, z_hi, x, y, z_lo):
    at = lambda y2, z2: device(half, z_hi, x, y2, z2)
    children = [
        ((z_lo == 0) & (y <= 1), at(y + 1, 0)),
        ((z_lo == 0) & (y == 0), at(3, 0)),
        ((y >= 1) & (z_lo < 3), at(y, z_lo + 1)),
        ((y == 1) & (z_lo >= 1), at(0, z_lo)),
    ]
    back = (y == 0) & (z_lo >= 1)
    parent_y = jnp.where(z_lo == 0, jnp.where(y == 2, 1, 0), jnp.where(y == 0, 1, y))
    parent_z = jnp.where((z_lo == 0) | back, z_lo, z_lo - 1)
    turn = jnp.where(y == 3, 1, y)
    hops = jnp.where(back, z_lo + 2, turn + z_lo)
    return children, at(parent_y, parent_z), hops


def count(children):
    total = 0
    for cond, _ in children:
        total = total + cond.astype(jnp.int32)
    return total


def wait_for(barrier, signals):
    @pl.when(signals > 0)
    def _():
        pl.semaphore_wait(barrier, signals)


def remote(src, dst, send, recv, target):
    return pltpu.make_async_remote_copy(
        src_ref=src, dst_ref=dst, send_sem=send, recv_sem=recv, device_id=target, device_id_type=MESH
    )


def split(value):
    high = value.astype(BF16)
    return high, (value - high.astype(F32)).astype(BF16)


def outer(left, right):
    left_high, left_low = split(left)
    right_high, right_low = split(right)
    dims = ((1,), (1,))
    return dot(left_high, right_high, dims) + (dot(left_high, right_low, dims) + dot(left_low, right_high, dims))


def panel_kernel(a_ref, inv_ref, f_ref, d_ref, l_ref, send, recv, own):
    half, z_hi, x, y, z_lo = place()
    source, children, parent, _ = group_tree(half, z_hi, x, y, z_lo, 0, 0, 0)
    active = (y == 0) & (z_lo == 0)
    barrier = pltpu.get_barrier_semaphore()

    @pl.when(active)
    def _():
        @pl.when(jnp.logical_not(source))
        def _():
            pl.semaphore_signal(barrier, inc=1, device_id=parent, device_id_type=MESH)

        wait_for(barrier, count(children))

        def piece(ref, block):
            return ref.at[pl.ds(block * WIDTH, WIDTH), pl.ds(0, block * WIDTH)]

        def copy(block, number, src=d_ref):
            return remote(
                piece(src, block), piece(d_ref, block), send.at[number, block - 1], recv.at[block - 1], children[number][1]
            )

        def mine(block):
            return pltpu.make_async_copy(piece(a_ref, block), piece(d_ref, block), own.at[block - 1])

        @pl.when(source)
        def _():
            for block in range(1, BLOCKS):
                for number in range(len(children)):
                    copy(block, number, a_ref).start()
                mine(block).start()

        lower = lax.broadcasted_iota(jnp.int32, (WIDTH, WIDTH), 0) >= lax.broadcasted_iota(jnp.int32, (WIDTH, WIDTH), 1)
        f_ref[:, :WIDTH] = outer(a_ref[:, :WIDTH], jnp.where(lower, inv_ref[0], 0.0))

        @pl.when(source)
        def _():
            for block in range(1, BLOCKS):
                mine(block).wait()

        @pl.when(jnp.logical_not(source))
        def _():
            for block in range(1, BLOCKS):
                copy(block, 0).wait_recv()
                for number, (cond, _) in enumerate(children):
                    @pl.when(cond)
                    def _():
                        copy(block, number).start()

        for block in range(BLOCKS):
            inverse = jnp.where(lower, inv_ref[block], 0.0)
            here = pl.ds(block * WIDTH, WIDTH)
            done = pl.ds(0, block * WIDTH)
            if block > 0:
                above = l_ref[here, done]
                f_ref[:, here] = outer(a_ref[:, here] - outer(f_ref[:, done], above), inverse)
            if block + 1 < BLOCKS:
                below = pl.ds((block + 1) * WIDTH, PANEL - (block + 1) * WIDTH)
                current = d_ref[below, here]
                if block > 0:
                    current = current - outer(l_ref[below, done], above)
                l_ref[below, here] = outer(current, inverse)

        for block in range(1, BLOCKS):
            for number, (cond, _) in enumerate(children):
                @pl.when(cond)
                def _():
                    copy(block, number).wait_send()


def panel(a, inverse_blocks):
    return pl.pallas_call(
        panel_kernel,
        out_shape=jax.ShapeDtypeStruct(a.shape, F32),
        in_specs=[pl.BlockSpec(memory_space=pltpu.VMEM)] * 2,
        out_specs=pl.BlockSpec(memory_space=pltpu.VMEM),
        scratch_shapes=[
            pltpu.VMEM((PANEL, PANEL), F32),
            pltpu.VMEM((PANEL, PANEL), F32),
            pltpu.SemaphoreType.DMA((4, BLOCKS - 1)),
            pltpu.SemaphoreType.DMA((BLOCKS - 1,)),
            pltpu.SemaphoreType.DMA((BLOCKS - 1,)),
        ],
        compiler_params=pltpu.CompilerParams(collective_id=0, has_side_effects=True, vmem_limit_bytes=24 * 2**20),
        name="panel",
    )(a, inverse_blocks)


CHUNK = 32
STEP = 2


def spread_kernel(f_ref, row_ref, col_ref, recv_z, recv_y, recv_g, send_z, send_y, send_g, own):
    half, z_hi, x, y, z_lo = place()
    side = row_ref.shape[0] // 2
    chunks = side // CHUNK
    tree_z, parent_z, hops_z = z_first_tree(half, z_hi, x, y, z_lo)
    tree_y, parent_y, hops_y = y_first_tree(half, z_hi, x, y, z_lo)
    root = (y == 0) & (z_lo == 0)
    lead, near = half == y // 2, z_hi == y % 2
    source = lead & near & (x == z_lo)
    column = [
        device(half, 1 - z_hi, x, y, z_lo),
        device(half, z_hi, (x + 1) % 4, y, z_lo),
        device(half, z_hi, (x + 3) % 4, y, z_lo),
        device(1 - half, z_hi, x, y, z_lo),
    ]
    barrier = pltpu.get_barrier_semaphore()

    @pl.when(jnp.logical_not(root))
    def _():
        pl.semaphore_signal(barrier, inc=1, device_id=parent_z, device_id_type=MESH)
        pl.semaphore_signal(barrier, inc=1, device_id=parent_y, device_id_type=MESH)

    for target in column:
        pl.semaphore_signal(barrier, inc=1, device_id=target, device_id_type=MESH)

    @pl.when(root)
    def _():
        mine = pltpu.make_async_copy(f_ref, row_ref, own)
        mine.start()
        mine.wait()

    pl.semaphore_wait(barrier, count(tree_z) + count(tree_y) + len(column))

    def rows(number):
        return pl.ds(pl.multiple_of(number * CHUNK, CHUNK), CHUNK)

    def forward(src, dst, number, tree, sends, recv):
        for slot, (cond, target) in enumerate(tree):
            @pl.when(cond)
            def _():
                remote(src.at[rows(number)], dst.at[rows(number)], sends(slot), recv, target).start()

    def turn(away):
        return jnp.where(away == 3, 1, away)

    def column_tree(bridge):
        from_source = (x - z_lo + 4) % 4
        away = jnp.where(near, from_source, (from_source - bridge + 4) % 4)
        children = [
            (lead & near & (from_source == bridge), column[0]),
            (lead & (away <= 1), column[1]),
            (lead & (away == 0), column[2]),
            (lead, column[3]),
        ]
        hops = turn(away) + jnp.where(lead, 0, 1) + jnp.where(near, 0, 2 + turn(bridge))
        return children, hops

    def along_row(number, offset, tree, sends, recv):
        @pl.when((number >= 0) & (number < chunks))
        def _():
            @pl.when(jnp.logical_not(root))
            def _():
                at = row_ref.at[rows(offset + number)]
                remote(at, at, sends.at[0], recv.at[number], tree[0][1]).wait_recv()

            forward(row_ref, row_ref, offset + number, tree, lambda slot: sends.at[slot], recv.at[number])

            @pl.when(source)
            def _():
                along = offset + number
                forward(row_ref, col_ref, along, column_tree(number % 4)[0], lambda slot: send_g.at[slot, along], recv_g.at[along])

    def along_col(step, offset):
        def one(bridge, carry):
            children, hops = column_tree(bridge)
            number = step - hops * STEP

            @pl.when((number >= 0) & (number < chunks) & (number % 4 == bridge) & jnp.logical_not(source))
            def _():
                along = offset + number
                at = col_ref.at[rows(along)]
                remote(at, at, send_g.at[0, along], recv_g.at[along], column[0]).wait_recv()
                forward(col_ref, col_ref, along, children, lambda slot: send_g.at[slot, along], recv_g.at[along])

            return carry

        lax.fori_loop(0, 4, one, 0)

    start_z, start_y = hops_z * STEP, hops_y * STEP

    def body(step, carry):
        along_row(step - start_z, 0, tree_z, send_z, recv_z)
        along_row(step - start_y, chunks, tree_y, send_y, recv_y)
        along_col(step - start_z, 0)
        along_col(step - start_y, chunks)
        return carry

    lax.fori_loop(0, chunks + STEP * 13, body, 0)

    @pl.when(source)
    def _():
        mine = pltpu.make_async_copy(row_ref, col_ref, own)
        mine.start()
        mine.wait()

    def drain(tree, sends):
        at = row_ref.at[pl.ds(0, side)]
        for slot, (cond, target) in enumerate(tree):
            @pl.when(cond)
            def _():
                remote(at, at, sends.at[slot], recv_z.at[0], target).wait_send()

    drain(tree_z, send_z)
    drain(tree_y, send_y)

    def drain_column(number, carry):
        at = row_ref.at[rows(number)]
        for slot, (cond, target) in enumerate(column_tree(number % 4)[0]):
            @pl.when(cond)
            def _():
                remote(at, at, send_g.at[slot, number], recv_z.at[0], target).wait_send()

        return carry

    lax.fori_loop(0, 2 * chunks, drain_column, 0)


def spread(f):
    chunks = f.shape[0] // 2 // CHUNK
    return pl.pallas_call(
        spread_kernel,
        out_shape=[jax.ShapeDtypeStruct(f.shape, F32)] * 2,
        in_specs=[pl.BlockSpec(memory_space=pltpu.VMEM)],
        out_specs=[pl.BlockSpec(memory_space=pltpu.VMEM)] * 2,
        scratch_shapes=[
            pltpu.SemaphoreType.DMA((chunks,)),
            pltpu.SemaphoreType.DMA((chunks,)),
            pltpu.SemaphoreType.DMA((2 * chunks,)),
            pltpu.SemaphoreType.DMA((4,)),
            pltpu.SemaphoreType.DMA((4,)),
            pltpu.SemaphoreType.DMA((4, 2 * chunks)),
            pltpu.SemaphoreType.DMA,
        ],
        compiler_params=pltpu.CompilerParams(collective_id=1, has_side_effects=True, vmem_limit_bytes=24 * 2**20),
        name="spread",
    )(f)


def exchange_kernel(
    x_ref, parent_ref, maps_ref, out_ref, panel_ref,
    col_ref, row_land_ref, col_land_ref, upper, held, strained, passed, packed, landed, pick, by_col, parts, by_row, put,
    own, first, ring_sent, ring_got, less_sent, less_got, sent, got, kept,
):
    half, z_hi, x, y, z_lo = place()
    z = z_hi * 4 + z_lo
    mid = held.shape[1] // 2
    tile = 256
    rows_dims = ((1,), (1,))
    up, down = (z + 1) % 8, (z + 7) % 8
    above = device(half, up // 4, x, y, up % 4)
    below = device(half, down // 4, x, y, down % 4)

    def peer(number):
        return device((half + number // 16) % 2, z_hi, (x + number // 4) % 4, (y + number) % 4, z_lo)

    mine = pltpu.make_async_copy(x_ref, held.at[0], own)
    mine.start()
    front = pltpu.make_async_copy(parent_ref, out_ref, first)
    front.start()
    barrier = pltpu.get_barrier_semaphore()
    for target in (above, below):
        pl.semaphore_signal(barrier, inc=1, device_id=target, device_id_type=MESH)

    def greet(number, carry):
        pl.semaphore_signal(barrier, inc=1, device_id=peer(number), device_id_type=MESH)
        return carry

    lax.fori_loop(1, 32, greet, 0)
    mine.wait()
    pl.semaphore_wait(barrier, 33)

    def at_of(number):
        return jnp.where(number % 2 == 1, 8 - (number + 1) // 2, number // 2)

    def spot(at):
        return at - at // 7 * 3

    def part(at, side):
        return held.at[spot(at), pl.ds(side * mid, mid), :]


    def ring(at, way, side):
        to = (at + 7) % 8 if way == 0 else (at + 1) % 8
        return remote(
            part(at, side), part(to, side), ring_sent.at[way, at, side], ring_got.at[to, side], (above, below)[way]
        )

    def arrived(at, side):
        remote(part(at, side), part(at, side), ring_sent.at[0, at, side], ring_got.at[at, side], above).wait_recv()

    def less(place, way):
        return remote(
            passed.at[place], strained.at[place], less_sent.at[place], less_got.at[place], (above, below)[way]
        )

    def columns_of(which, at, here):
        slots = lax.broadcasted_iota(jnp.int32, (4 * CAP, SUB), 0)
        col_pick = (slots == col_ref[which, (z + at) % 4]).astype(F32).astype(BF16)
        high, low = split(held[spot(at), here, :])
        return dot(col_pick, high, rows_dims), dot(col_pick, low, rows_dims)

    def strain(at, side, way, place):
        high, low = columns_of(1 + way, at, pl.ds(side * mid, mid))
        passed[place] = high + low
        less(place, way).start()

    def message(number, to):
        to_half, to_x, to_y = (half + to // 16) % 2, (x + to // 4) % 4, (y + to) % 4
        src = packed.at[
            number % 4,
            pl.ds(pl.multiple_of(to_y * CAP, CAP), CAP),
            pl.ds(pl.multiple_of((to_half * 4 + to_x) * 128, 128), 128),
        ]
        dst = landed.at[
            at_of(number), half, pl.ds(pl.multiple_of(y * CAP, CAP), CAP), pl.ds(pl.multiple_of(x * 128, 128), 128)
        ]
        return src, dst

    def deliver(number):
        src, dst = message(number, 0)
        pltpu.make_async_copy(src, dst, kept.at[number]).start()

        def one(to, carry):
            src, dst = message(number, to)
            remote(src, dst, sent.at[number], got.at[number], peer(to)).start()
            return carry

        lax.fori_loop(1, 32, one, 0)

    def others():
        return out_ref.at[pl.ds(0, 31 * 8), :]

    def gone(number):
        remote(others(), others(), sent.at[number], got.at[number], above).wait_send()

    def landed_all(number):
        remote(others(), others(), sent.at[number], got.at[number], above).wait_recv()
        src, dst = message(number, 0)
        pltpu.make_async_copy(src, dst, kept.at[number]).wait()

    def pack(number):
        at = at_of(number)
        there = (z + at) % 8
        for side in range(2):
            lanes = pl.ds(side * mid, mid)
            full = (at != 4) & (at != (3, 5)[side])

            @pl.when(full)
            def _():
                high, low = columns_of(0, at, lanes)
                by_col[: 4 * CAP, lanes] = high.astype(BF16)
                by_col[4 * CAP :, lanes] = low.astype(BF16)

            @pl.when(jnp.logical_not(full))
            def _():
                high, low = split(strained[jnp.where(at == 4, 2 + side, 1 - side)])
                by_col[: 4 * CAP, lanes] = high
                by_col[4 * CAP :, lanes] = low

        def rows(step, carry):
            here = pl.ds(pl.multiple_of(step * tile, tile), tile)
            both = dot(by_col[...], pick[there // 4, here, :], rows_dims)
            packed[number % 4, :, here] = both[: 4 * CAP] + both[4 * CAP :]
            return carry

        lax.fori_loop(0, LOC // tile, rows, 0)

    def rows_of(number, child, step):
        source = (z + at_of(number)) % 8 // 4
        places = lax.broadcasted_iota(jnp.int32, (tile, SUB), 0) + step * tile
        row_put = (places == row_land_ref[child, source]).astype(F32).astype(BF16)
        return dot(row_put, parts[child], rows_dims).astype(BF16)

    def take(number):
        landed_all(number)
        for child in range(2):
            high, low = split(landed[at_of(number), child])
            parts[child, : 4 * CAP] = high
            parts[child, 4 * CAP :] = low

    def unpack_first(number):
        take(number)

        def rows(step, carry):
            here = pl.ds(pl.multiple_of(step * tile, tile), tile)
            for child in range(2):
                by_row[at_of(number) % 4, child, here, :] = rows_of(number, child, step)
            return carry

        lax.fori_loop(0, LOC // tile, rows, 0)

    def unpack_second(number, carry):
        source = (z + at_of(number)) % 4
        for child in range(2):
            places = lax.broadcasted_iota(jnp.int32, (LOC, 4 * CAP), 0)
            col_put = (places == col_land_ref[child, source]).astype(F32).astype(BF16)
            put[child, :, : 4 * CAP] = col_put
            put[child, :, 4 * CAP :] = col_put
        take(number)

        def rows(step, carry):
            here = pl.ds(pl.multiple_of(step * tile, tile), tile)
            total = out_ref[here, :]
            for child in range(2):
                both = by_row[at_of(number) % 4, child, here, :] + rows_of(number, child, step)
                total = total + dot(both, put[child], rows_dims)
            out_ref[here, :] = total
            panel_ref[here, :] = total[:, :PANEL]
            return carry

        lax.fori_loop(0, LOC // tile, rows, 0)
        return carry

    for turn in range(2):
        for way in range(2):
            ring(0, way, (turn + way) % 2).start()
    upper[...] = (
        lax.broadcasted_iota(jnp.int32, (SUB, SUB), 0) < lax.broadcasted_iota(jnp.int32, (SUB, SUB), 1)
    ).astype(F32).astype(BF16)

    def before(member):
        return dot(member.astype(F32).astype(BF16), upper[...], ((1,), (0,)))

    def entries(block):
        return maps_ref[pl.ds(half, 1), pl.ds(pl.multiple_of(block * SUB, SUB), SUB)]

    def send_slots(parents):
        targets = parents >> 10
        member = targets == lax.broadcasted_iota(jnp.int32, (GROUPS, SUB), 0)
        rank = jnp.sum(jnp.where(member, before(member), 0.0), axis=0, keepdims=True)
        return targets, rank.astype(jnp.int32)

    for source in range(2):
        for sub in range(2):
            targets, rank = send_slots(entries(source * 8 + x * 2 + sub))
            slot = (((targets >> 3) * 4 + (targets & 3)) * 2 + sub) * CAP + rank
            slot = jnp.where(((targets >> 2) & 1) == z_hi, slot, -1)
            slots = lax.broadcasted_iota(jnp.int32, (LOC, SUB), 0)
            pick[source, :, sub * SUB : (sub + 1) * SUB] = (slots == slot).astype(F32).astype(BF16)
    for source in range(4):
        targets, rank = send_slots(entries(y * 4 + source))
        for which, stop in enumerate((0, 1, 3)):
            slot = (targets >> 2) * CAP + rank
            col_ref[which, source] = jnp.where((targets & 3) == (z_lo + stop) % 4, slot, -1)

    def landing(child, mine, store):
        parents = jnp.concatenate(
            [maps_ref[child : child + 1, block * SUB : (block + 1) * SUB] for block in range(GROUPS)], axis=0
        )
        member = (parents >> 10) == mine
        rank = jnp.where(member, before(member).astype(jnp.int32), -1)
        place = (parents & (LOC - 1)) + 1
        slots = lax.broadcasted_iota(jnp.int32, (2 * CAP, SUB), 0)
        line = lax.broadcasted_iota(jnp.int32, (8, SUB), 0)

        def side(block, shift):
            values = place[block : block + 1]
            values = jnp.where(line == 0, values >> 5, jnp.where(line == 1, values & 31, 0)).astype(F32).astype(BF16)
            mine_rank = rank[block : block + 1]
            hit = slots == jnp.where(mine_rank < 0, -1, mine_rank + shift)
            return dot(values, hit.astype(F32).astype(BF16), rows_dims)

        store(lambda first, second: (lambda both: (both[0:1] * 32.0 + both[1:2]).astype(jnp.int32) - 1)(
            side(first, 0) + side(second, CAP)
        ))

    for child in range(2):
        def rows_land(pair):
            for source in range(2):
                for at_x in range(4):
                    block = source * 8 + at_x * 2
                    row_land_ref[child, source, :, at_x * 128 : (at_x + 1) * 128] = pair(block, block + 1)

        def cols_land(pair):
            for source in range(4):
                for at_y in range(2):
                    col_land_ref[child, source, :, at_y * 128 : (at_y + 1) * 128] = pair(
                        at_y * 8 + source, at_y * 8 + 4 + source
                    )

        landing(child, half * 8 + z_hi * 4 + x, rows_land)
        landing(child, y * 4 + z_lo, cols_land)
    front.wait()

    def event(number, carry):
        @pl.when(number == 1)
        def _():
            for turn in range(2):
                for way in range(2):
                    at, side = (7, 1)[way], (turn + way) % 2
                    arrived(at, side)
                    ring(at, way, side).start()

        @pl.when(number == 3)
        def _():
            for way in range(2):
                at, side = (6, 2)[way], way
                arrived(at, side)
                ring(at, way, side).start()
            for way in range(2):
                at, side = (6, 2)[way], 1 - way
                arrived(at, side)
                strain(at, side, way, way)

        @pl.when(number == 5)
        def _():
            for way in range(2):
                at, side = (5, 3)[way], way
                arrived(at, side)
                strain(at, side, way, 2 + way)
            for way in range(2):
                less(way, way).wait_recv()

        @pl.when(number == 7)
        def _():
            for way in range(2):
                less(2 + way, way).wait_recv()

        @pl.when(number >= 4)
        def _():
            gone(number - 4)

        pack(number)

        deliver(number)

        @pl.when((number >= 3) & (number < 7))
        def _():
            unpack_first(number - 3)

        return carry

    lax.fori_loop(0, 8, event, 0)
    lax.fori_loop(4, 8, unpack_second, 0)

    def settle(number, carry):
        gone(number)
        return carry

    lax.fori_loop(4, 8, settle, 0)
    for way in range(2):
        for at in ((0, 7), (0, 1))[way]:
            for side in range(2):
                ring(at, way, side).wait_send()
        ring((6, 2)[way], way, way).wait_send()
        less(way, way).wait_send()
        less(2 + way, way).wait_send()


def exchange(block, parent, maps):
    rows, cols = block.shape
    return pl.pallas_call(
        exchange_kernel,
        out_shape=[jax.ShapeDtypeStruct(parent.shape, F32), jax.ShapeDtypeStruct((LOC, PANEL), F32)],
        in_specs=[pl.BlockSpec(memory_space=pl.ANY)] * 2 + [pl.BlockSpec(memory_space=pltpu.VMEM)],
        out_specs=[pl.BlockSpec(memory_space=pltpu.VMEM)] * 2,
        scratch_shapes=[
            pltpu.VMEM((3, 4, 1, SUB), jnp.int32),
            pltpu.VMEM((2, 2, 1, SUB), jnp.int32),
            pltpu.VMEM((2, 4, 1, 4 * CAP), jnp.int32),
            pltpu.VMEM((SUB, SUB), BF16),
            pltpu.VMEM((7, rows, cols), F32),
            pltpu.VMEM((4, 4 * CAP, SUB), F32),
            pltpu.VMEM((4, 4 * CAP, SUB), F32),
            pltpu.VMEM((4, 4 * CAP, LOC), F32),
            pltpu.VMEM((8, 2, 4 * CAP, SUB), F32),
            pltpu.VMEM((2, LOC, rows), BF16),
            pltpu.VMEM((8 * CAP, LOC), BF16),
            pltpu.VMEM((2, 8 * CAP, SUB), BF16),
            pltpu.VMEM((4, 2, LOC, 8 * CAP), BF16),
            pltpu.VMEM((2, LOC, 8 * CAP), BF16),
            pltpu.SemaphoreType.DMA,
            pltpu.SemaphoreType.DMA,
            pltpu.SemaphoreType.DMA((2, 8, 2)),
            pltpu.SemaphoreType.DMA((8, 2)),
            pltpu.SemaphoreType.DMA((4,)),
            pltpu.SemaphoreType.DMA((4,)),
            pltpu.SemaphoreType.DMA((8,)),
            pltpu.SemaphoreType.DMA((8,)),
            pltpu.SemaphoreType.DMA((8,)),
        ],
        compiler_params=pltpu.CompilerParams(collective_id=2, has_side_effects=True, vmem_limit_bytes=63 * 2**20),
        name="exchange",
    )(block, parent, maps)


def local(parent_front, child_blocks, row_maps, inverse_blocks):
    assembled, columns = exchange(child_blocks[0], parent_front, row_maps)
    factor = panel(columns, inverse_blocks)
    factor_rows, factor_cols = spread(factor)
    product = lax.dot_general(
        factor_rows, factor_cols, (((1,), (1,)), ((), ())), precision=lax.Precision.HIGH, preferred_element_type=F32
    )
    return assembled - product, factor_rows.astype(BF16)


def solution(mesh):
    in_specs = (P(("half", "row"), "col"), P("half", "row", "col"), P(), P())
    out_specs = (P(("half", "row"), "col"), P(("half", "row"), None))
    return jax.shard_map(local, mesh=mesh, in_specs=in_specs, out_specs=out_specs, check_vma=False)
```
